512 devices in a mesh: ctx: 16 (over z), head: 8 (over y, core), seq: 4 (over x).
Axes of the slice: x: 4, y: 4, z: 16, core: 2. Of those that a mesh axis runs over, the one named last changes fastest.
Arguments:
- x_heads: bfloat16 [4, 64, 4096, 128], P('seq', 'head', 'ctx'), may hold values from -6 to 6
- target: bfloat16 [4, 64, 4096, 128], P('seq', 'head', 'ctx'), may hold values from -6 to 6
- b_proj: bfloat16 [4, 4096, 128], P('seq', 'ctx'), may hold values from -6 to 6
- c_proj: bfloat16 [4, 4096, 128], P('seq', 'ctx'), may hold values from -0.5 to 0.5
- dt_raw: float32 [4, 64, 4096], P('seq', 'head', 'ctx'), may hold values from -1.2 to 1.2
- a_log: float32 [64], P('head'), as said below
- skip_gain: float32 [64], P('head'), may hold values from 0.5 to 1.5
- dt_bias: float32 [64], P('head'), may hold values from -4.5 to -3.5
Outputs:
- grad_x: bfloat16 [4, 64, 4096, 128], P('seq', 'head', 'ctx')
- grad_b: float32 [4, 4096, 128], P('seq', ('ctx', 'head'))
- grad_c: float32 [4, 4096, 128], P('seq', ('ctx', 'head'))
- grad_dt_raw: float32 [4, 64, 4096], P('seq', 'head', 'ctx')
- grad_a_log: float32 [64], P('head')
- grad_skip: float32 [64], P('head')
- grad_dt_bias: float32 [64], P('head')
The draws below stay inside these ranges and needn't reach their ends.
Inputs may be any that keep to these rules, and one draw needn't show every extreme that they name: exp(a_log) lies between 16 / 4096 and 3.
All inputs are finite; a program needn't handle non-finite values.
Results may differ from the reference program's by a relative error of at most 0.0054.
Values sent between devices are 32-bit elements; how exact they have to be, the bound alone decides.
A program may use at most 64 MiB of HBM per device.

```python
import math
from functools import partial
import jax
import jax.numpy as jnp
from jax import lax

P_SIZE = 128
N = 128
GROUP = 256
HEADS = 64
SEQUENCE_LENGTH = 4096
SEQS = 4


def draw_a_log(key, part):
    pick_key, slow_key, fast_key = jax.random.split(jax.random.fold_in(key, 11), 3)
    slow_heads = jax.random.bernoulli(pick_key, 0.5, (HEADS,))
    slow_values = jax.random.uniform(slow_key, (HEADS,), jnp.float32, math.log(16.0) - math.log(SEQUENCE_LENGTH), math.log(48.0) - math.log(SEQUENCE_LENGTH))
    fast_values = jax.random.uniform(fast_key, (HEADS,), jnp.float32, math.log(0.5), math.log(3.0))
    return jnp.where(slow_heads, slow_values, fast_values)


def draw_dt_raw(key, part):
    baseline_random_key, jitter_random_key = jax.random.split(jax.random.fold_in(key, 23), 2)
    complete_shape = (SEQS, HEADS, SEQUENCE_LENGTH)
    baseline_values = jax.random.uniform(baseline_random_key, (SEQS, HEADS, SEQUENCE_LENGTH // GROUP, 1), jnp.float32, -0.7, 0.7)
    baseline_values = jnp.broadcast_to(baseline_values, (SEQS, HEADS, SEQUENCE_LENGTH // GROUP, GROUP)).reshape(complete_shape)
    jitter_component = jnp.clip(0.4 * jax.random.normal(jitter_random_key, complete_shape, jnp.float32), -0.8, 0.8)
    return jnp.clip(baseline_values + jitter_component, -1.2, 1.2)


def levels(stream_key, dims, shards, smallest, high):
    factor_of = 1.0
    for axis_at, shards_of in shards:
        heights = jax.random.uniform(jax.random.fold_in(jax.random.fold_in(stream_key, 6), axis_at), (shards_of,), jnp.float32, smallest / len(shards), high / len(shards))
        factor_of = factor_of * jnp.repeat(jnp.exp(heights), dims[axis_at] // shards_of).reshape((-1,) + (1,) * (len(dims) - 1 - axis_at))
    return factor_of


def gaussian(own_key, extent, spread, limit, shards=(), held_as=jnp.bfloat16):
    level = levels(own_key, extent, shards, -0.22, 0.18) if shards else 1.0
    entries = jax.random.normal(own_key, extent, jnp.float32) * spread * level
    return jnp.minimum(jnp.maximum(entries, -limit), limit).astype(held_as)


def setup_inputs(seed: int = 0) -> dict:
    arg_keys = jax.random.split(jax.random.key(seed), 9)
    x_heads = gaussian(arg_keys[0], (SEQS, HEADS, SEQUENCE_LENGTH, P_SIZE), 1.0, 6.0, ((0, 4), (1, 8), (2, 16)))
    target = gaussian(arg_keys[1], (SEQS, HEADS, SEQUENCE_LENGTH, P_SIZE), 1.0, 6.0, ((0, 4), (1, 8), (2, 16)))
    b_proj = gaussian(arg_keys[2], (SEQS, SEQUENCE_LENGTH, N), 1.0, 6.0, ((0, 4), (1, 16)))
    c_proj = gaussian(arg_keys[3], (SEQS, SEQUENCE_LENGTH, N), N ** -0.5, 0.5, ((0, 4), (1, 16)))
    dt_raw = draw_dt_raw(jax.random.fold_in(arg_keys[8], 71), 0)
    a_log = draw_a_log(jax.random.fold_in(arg_keys[8], 71), 0)
    skip_gain = jnp.clip(0.5 + 1.0 * jax.random.uniform(arg_keys[6], (HEADS,), jnp.float32) ** levels(arg_keys[6], (HEADS,), ((0, 8),), -0.2, 0.2), 0.5, 1.5)
    dt_bias = jnp.clip(-4.5 + 1.0 * jax.random.uniform(arg_keys[7], (HEADS,), jnp.float32) ** levels(arg_keys[7], (HEADS,), ((0, 8),), -0.2, 0.2), -4.5, -3.5)
    return dict(x_heads=x_heads, target=target, b_proj=b_proj, c_proj=c_proj, dt_raw=dt_raw, a_log=a_log, skip_gain=skip_gain, dt_bias=dt_bias)


highest = lax.Precision.HIGHEST


def block_logs(dt_block, decay_rate):
    return jnp.cumsum(-decay_rate[:, None] * dt_block, axis=-1)


def state_part(x_block, b_block, dt_block, log_decay):
    weights = jnp.exp(log_decay[:, -1:] - log_decay) * dt_block
    scaled = (x_block.astype(jnp.float32) * weights[:, :, None]).astype(jnp.bfloat16)
    contrib = jnp.einsum("hjp,jn->hpn", scaled, b_block, preferred_element_type=jnp.float32)
    return weights, scaled, contrib, jnp.exp(log_decay[:, -1])


def intra_parts(b_block, c_block, dt_block, log_decay):
    block_size = log_decay.shape[-1]
    row_ids = lax.broadcasted_iota(jnp.int32, (block_size, block_size), 0)
    column_ids = lax.broadcasted_iota(jnp.int32, (block_size, block_size), 1)
    causal = (row_ids >= column_ids)[None]
    log_gaps = log_decay[:, :, None] - log_decay[:, None, :]
    decays = jnp.where(causal, jnp.exp(jnp.where(causal, log_gaps, 0.0)), 0.0)
    scores = jnp.einsum("in,jn->ij", c_block, b_block, preferred_element_type=jnp.float32)
    mixing = (scores[None] * decays * dt_block[:, None, :]).astype(jnp.bfloat16)
    return decays, scores, mixing


def forward_block(x_block, t_block, c_block, log_decay, skip_gain, start_state, mixing):
    inner = jnp.einsum("hij,hjp->hip", mixing, x_block, preferred_element_type=jnp.float32)
    state_low = start_state.astype(jnp.bfloat16)
    growth = jnp.exp(log_decay)[:, :, None]
    carried = jnp.einsum("in,hpn->hip", c_block, state_low, preferred_element_type=jnp.float32) * growth
    out_error = inner + carried + skip_gain[:, None, None] * x_block.astype(jnp.float32) - t_block.astype(jnp.float32)
    error_weighted = (out_error * growth).astype(jnp.bfloat16)
    pulled = jnp.einsum("hip,in->hpn", error_weighted, c_block, preferred_element_type=jnp.float32)
    return out_error, carried, error_weighted, state_low, pulled


def backward_local(x_block, b_block, c_block, dt_block, skip_gain, out_error, carried, error_weighted, state_low, decays, scores, mixing):
    error_low = out_error.astype(jnp.bfloat16)
    grad_mixing = jnp.einsum("hip,hjp->hij", error_low, x_block, preferred_element_type=jnp.float32)
    grad_in = jnp.einsum("hij,hip->hjp", mixing, error_low, preferred_element_type=jnp.float32) + skip_gain[:, None, None] * out_error
    masked = grad_mixing * decays
    grad_score = (masked * dt_block[:, None, :]).astype(jnp.bfloat16)
    grad_c = jnp.einsum("hij,jn->in", grad_score, b_block, preferred_element_type=jnp.float32)
    grad_c = grad_c + jnp.einsum("hip,hpn->in", error_weighted, state_low, preferred_element_type=jnp.float32)
    grad_b = jnp.einsum("hij,in->jn", grad_score, c_block, preferred_element_type=jnp.float32)
    product = masked * scores[None]
    column_sum = jnp.sum(product, axis=1)
    row_sum = jnp.einsum("hij,hj->hi", product, dt_block, precision=highest)
    grad_logs = row_sum - column_sum * dt_block + jnp.sum(out_error * carried, axis=-1)
    grad_skip = jnp.sum(out_error * x_block.astype(jnp.float32), axis=(1, 2))
    return grad_in, grad_c, grad_b, column_sum, grad_logs, grad_skip


def backward_state(x_block, b_block, log_decay, weights, scaled, start_state, end_adjoint):
    adjoint_low = end_adjoint.astype(jnp.bfloat16)
    grad_b = jnp.einsum("hjp,hpn->jn", scaled, adjoint_low, preferred_element_type=jnp.float32)
    grad_scaled = jnp.einsum("jn,hpn->hjp", b_block, adjoint_low, preferred_element_type=jnp.float32)
    grad_in = grad_scaled * weights[:, :, None]
    grad_weight = jnp.sum(grad_scaled * x_block.astype(jnp.float32), axis=-1)
    grad_step = grad_weight * jnp.exp(log_decay[:, -1:] - log_decay)
    grad_logs = -grad_weight * weights
    grad_final = jnp.sum(grad_weight * weights, axis=-1) + jnp.exp(log_decay[:, -1]) * jnp.sum(end_adjoint * start_state, axis=(1, 2))
    return grad_in, grad_b, grad_step, grad_logs, grad_final


def finish_block(column_sum, grad_logs_a, grad_step_b, grad_logs_b, grad_final, dt_block, decay_rate):
    grad_logs = grad_logs_a + grad_logs_b
    grad_logs = grad_logs.at[:, -1].add(grad_final)
    grad_log_rate = jnp.flip(jnp.cumsum(jnp.flip(grad_logs, axis=-1), axis=-1), axis=-1)
    grad_step = column_sum + grad_step_b - decay_rate[:, None] * grad_log_rate
    grad_alog = -decay_rate * jnp.sum(grad_log_rate * dt_block, axis=-1)
    return grad_step, grad_alog


def one_sequence(decay_rate, skip_gain, dt_bias, seq_items):
    x_seq, t_seq, b_seq, c_seq, raw_seq = seq_items
    head_count, positions, head_size = x_seq.shape
    state_size = b_seq.shape[-1]
    block_count = positions // GROUP
    step_sizes = jax.nn.softplus(raw_seq + dt_bias[:, None])
    x_blocks = jnp.swapaxes(x_seq.reshape(head_count, block_count, GROUP, head_size), 0, 1)
    t_blocks = jnp.swapaxes(t_seq.reshape(head_count, block_count, GROUP, head_size), 0, 1)
    b_blocks = b_seq.reshape(block_count, GROUP, state_size)
    c_blocks = c_seq.reshape(block_count, GROUP, state_size)
    dt_blocks = jnp.swapaxes(step_sizes.reshape(head_count, block_count, GROUP), 0, 1)
    zero_state = jnp.zeros((head_count, head_size, state_size), jnp.float32)

    def forward(carry_state, block_items):
        x_block, t_block, b_block, c_block, dt_block = block_items
        log_decay = block_logs(dt_block, decay_rate)
        weights, scaled, contrib, decay_total = state_part(x_block, b_block, dt_block, log_decay)
        decays, scores, mixing = intra_parts(b_block, c_block, dt_block, log_decay)
        outputs = forward_block(x_block, t_block, c_block, log_decay, skip_gain, carry_state, mixing)
        return decay_total[:, None, None] * carry_state + contrib, (carry_state, outputs[4], decay_total)

    final_state, (start_states, pulled_all, decay_totals) = lax.scan(forward, zero_state, (x_blocks, t_blocks, b_blocks, c_blocks, dt_blocks))

    def reverse_chain(adjoint, chain_items):
        decay_total, pulled = chain_items
        return decay_total[:, None, None] * adjoint + pulled, adjoint

    first_adjoint, end_adjoints = lax.scan(reverse_chain, zero_state, (decay_totals, pulled_all), reverse=True)

    def gradients(block_items):
        x_block, t_block, b_block, c_block, dt_block, start_state, end_adjoint = block_items
        log_decay = block_logs(dt_block, decay_rate)
        weights, scaled, contrib, decay_total = state_part(x_block, b_block, dt_block, log_decay)
        decays, scores, mixing = intra_parts(b_block, c_block, dt_block, log_decay)
        out_error, carried, error_weighted, state_low, pulled = forward_block(x_block, t_block, c_block, log_decay, skip_gain, start_state, mixing)
        grad_in_a, grad_c, grad_b_a, column_sum, grad_logs_a, grad_skip = backward_local(x_block, b_block, c_block, dt_block, skip_gain, out_error, carried, error_weighted, state_low, decays, scores, mixing)
        grad_in_b, grad_b_b, grad_step_b, grad_logs_b, grad_final = backward_state(x_block, b_block, log_decay, weights, scaled, start_state, end_adjoint)
        grad_step, grad_alog = finish_block(column_sum, grad_logs_a, grad_step_b, grad_logs_b, grad_final, dt_block, decay_rate)
        return (grad_in_a + grad_in_b).astype(jnp.bfloat16), grad_b_a + grad_b_b, grad_c, grad_step, grad_alog, grad_skip

    results = lax.map(gradients, (x_blocks, t_blocks, b_blocks, c_blocks, dt_blocks, start_states, end_adjoints))
    grad_x = jnp.swapaxes(results[0], 0, 1).reshape(head_count, positions, head_size)
    grad_b = results[1].reshape(positions, state_size)
    grad_c = results[2].reshape(positions, state_size)
    grad_step = jnp.swapaxes(results[3], 0, 1).reshape(head_count, positions)
    grad_raw = grad_step * jax.nn.sigmoid(raw_seq + dt_bias[:, None])
    return grad_x, grad_b, grad_c, grad_raw, jnp.sum(results[4], axis=0), jnp.sum(results[5], axis=0), jnp.sum(grad_raw, axis=1)


def reference(x_heads, target, b_proj, c_proj, dt_raw, a_log, skip_gain, dt_bias):
    decay_rate = jnp.exp(a_log)
    results = lax.map(partial(one_sequence, decay_rate, skip_gain, dt_bias), (x_heads, target, b_proj, c_proj, dt_raw))
    token_total = x_heads.shape[0] * x_heads.shape[2]
    grad_a_log = jnp.sum(results[4], axis=0) / token_total
    grad_skip = jnp.sum(results[5], axis=0) / (token_total * x_heads.shape[3])
    grad_dt_bias = jnp.sum(results[6], axis=0) / token_total
    return results[0], results[1], results[2], results[3], grad_a_log, grad_skip, grad_dt_bias
```

```python
import functools
import math

import jax
import jax.numpy as jnp
from jax import lax
from jax.experimental import pallas as pl
from jax.experimental.pallas import tpu as pltpu
from jax.sharding import PartitionSpec as P

LOG2E = math.log2(math.e)
PARTS = 2
HOP = (3, 2)
F32 = jnp.float32
BF16 = jnp.bfloat16
HIGHEST = lax.Precision.HIGHEST


def nn(a, b, precision=None):
    return lax.dot_general(a, b, (((1,), (0,)), ((), ())), precision=precision, preferred_element_type=F32)


def nt(a, b):
    return lax.dot_general(a, b, (((1,), (1,)), ((), ())), preferred_element_type=F32)


def tn(a, b):
    return lax.dot_general(a, b, (((0,), (0,)), ((), ())), preferred_element_type=F32)


def iota(shape, dim):
    return lax.broadcasted_iota(jnp.int32, shape, dim)


def column(ref, heads):
    eye = iota((heads, heads), 0) == iota((heads, heads), 1)
    spread = jnp.broadcast_to(ref[...], (heads, heads))
    return jnp.sum(jnp.where(eye, spread, 0.0), axis=1, keepdims=True)


def row_sums(values):
    high = values.astype(BF16)
    low = (values - high.astype(F32)).astype(BF16)
    both = jnp.concatenate([high, low], axis=1)
    return nt(jnp.ones((8, both.shape[1]), BF16), both)[0:1]


def kernel(
    sizes, x_ref, t_ref, b_ref, c_ref, dt_ref, alog_ref, skip_ref, bias_ref,
    gx_ref, gb_ref, gc_ref, gdt_ref, oalog_ref, oskip_ref, obias_ref,
    l_rows, r_rows, w_rows, g_rows, d_rows, lt_rows, s_rows, gl_rows, cq_rows, gf_rows, sk_rows,
    bt, ct, scores, cgt, decay, mixed, inner, g_cols, w_cols,
    contrib, srecv, snext, mbuf, wrecv, tbuf, pbuf, urecv,
    gst, gb_acc, gc_acc, rs_send, rs_recv, pz, px, pz_own, px_own,
    s_send, s_recv, w_send, w_recv, u_send, u_recv, rs_ss, rs_rs, pz_ss, pz_rs, px_ss, px_rs,
):
    nz, nh, ns = sizes
    heads, group, width = x_ref.shape[1:]
    state = b_ref.shape[2]
    piece = state // PARTS
    z = lax.axis_index("ctx")
    head_at = lax.axis_index("head")
    seq_at = lax.axis_index("seq")

    barrier = pltpu.get_barrier_semaphore()
    for name, at, count in (("ctx", z, nz), ("head", head_at, nh), ("seq", seq_at, ns)):
        for d in range(1, count):
            pl.semaphore_signal(
                barrier, inc=1, device_id={name: lax.rem(at + d, count)}, device_id_type=pl.DeviceIdType.MESH
            )

    rate = jnp.exp(column(alog_ref, heads))
    bias = column(bias_ref, heads)
    raw = dt_ref[0] + bias
    dt = jnp.maximum(raw, 0.0) + jnp.log1p(jnp.exp(-jnp.abs(raw)))
    upper = (iota((group, group), 0) <= iota((group, group), 1)).astype(F32)
    logs = nn(dt * (rate * -LOG2E), upper, HIGHEST)
    last = logs[:, group - 1 : group]
    rel = jnp.log(dt) * LOG2E - logs
    l_rows[...] = logs
    r_rows[...] = rel
    w_rows[...] = jnp.exp2(last + rel)
    g_rows[...] = jnp.exp2(logs)
    d_rows[...] = jnp.broadcast_to(jnp.exp2(last), (heads, width))
    lt_rows[...] = jnp.broadcast_to(last, (heads, width))
    s_rows[...] = jnp.broadcast_to(column(skip_ref, heads), (heads, width))
    bt[...] = b_ref[0].astype(F32).T
    ct[...] = c_ref[0].astype(F32).T
    scores[...] = nt(b_ref[0], c_ref[0])
    gst[...] = jnp.zeros_like(gst)
    gb_acc[...] = jnp.zeros_like(gb_acc)
    gc_acc[...] = jnp.zeros_like(gc_acc)

    pl.semaphore_wait(barrier, nz + nh + ns - 3)

    def chain(source, target, sends, receives, k, part, step):
        at = pl.ds(part * piece, piece)
        return pltpu.make_async_remote_copy(
            src_ref=source.at[k, at],
            dst_ref=target.at[k, at],
            send_sem=sends.at[k * PARTS + part],
            recv_sem=receives.at[k * PARTS + part],
            device_id={"ctx": lax.rem(z + step, nz)},
            device_id_type=pl.DeviceIdType.MESH,
        )

    def s_copy(k, part):
        return chain(snext, srecv, s_send, s_recv, k, part, 1)

    def w_copy(k, part):
        return chain(mbuf, wrecv, w_send, w_recv, k, part, nz - 1)

    def u_copy(k, part):
        return chain(pbuf, urecv, u_send, u_recv, k, part, nz - 1)

    def prepare(k):
        row = pl.ds(k, 1)
        contrib[k] = nn((bt[...] * w_rows[row, :]).astype(BF16), x_ref[0, k])
        scaled_c = (ct[...] * g_rows[row, :]).astype(BF16)
        cgt[...] = scaled_c
        mbuf[k] = nt(scaled_c, scaled_c)

    def pass_state(k):
        d = d_rows[pl.ds(k, 1), :]
        for part in range(PARTS):
            at = pl.ds(part * piece, piece)

            @pl.when(z > 0)
            def _():
                s_copy(k, part).wait_recv()
                snext[k, at] = d * srecv[k, at] + contrib[k, at]

            @pl.when(z == 0)
            def _():
                snext[k, at] = contrib[k, at]

            @pl.when(z < nz - 1)
            def _():
                s_copy(k, part).start()

        @pl.when(z == 0)
        def _():
            srecv[k] = jnp.zeros((state, width), F32)

    def pass_gram(k):
        d = d_rows[pl.ds(k, 1), :]
        for part in range(PARTS):
            at = pl.ds(part * piece, piece)

            @pl.when(z < nz - 1)
            def _():
                w_copy(k, part).wait_recv()
                mbuf[k, at] = (d * d) * wrecv[k, at] + mbuf[k, at]

            @pl.when(z > 0)
            def _():
                w_copy(k, part).start()

        @pl.when(z < nz - 1)
        def _():
            tbuf[k] = nn(wrecv[k], contrib[k], HIGHEST)

        @pl.when(z == nz - 1)
        def _():
            wrecv[k] = jnp.zeros((state, state), F32)
            urecv[k] = jnp.zeros((state, width), F32)

    def pass_adjoint(k):
        d = d_rows[pl.ds(k, 1), :]
        for part in range(PARTS):
            at = pl.ds(part * piece, piece)

            @pl.when(z < nz - 1)
            def _():
                u_copy(k, part).wait_recv()
                pbuf[k, at] = d * (urecv[k, at] + tbuf[k, at]) + pbuf[k, at]

            @pl.when(z > 0)
            def _():
                u_copy(k, part).start()

    def local(k):
        row = pl.ds(k, 1)
        logs_row = l_rows[row, :]
        rel_col = jnp.broadcast_to(r_rows[row, :], (width, group)).T
        logs_col = jnp.broadcast_to(logs_row, (width, group)).T
        g_cols[k] = jnp.exp2(logs_col)
        w_cols[k] = jnp.exp2(rel_col + lt_rows[row, :])
        gaps = jnp.concatenate([rel_col] * (group // width), axis=1) + logs_row
        causal = iota((group, group), 1) >= iota((group, group), 0)
        scaled_decay = jnp.exp2(jnp.where(causal, gaps, -1e30))
        decay[k] = scaled_decay
        mix = (scores[...] * scaled_decay).astype(BF16)
        mixed[k] = mix
        x = x_ref[0, k]
        within = tn(mix, x)
        inner[k] = within
        error = within + s_rows[row, :] * x.astype(F32) - t_ref[0, k].astype(F32)
        pbuf[k] = nn(cgt[...], error.astype(BF16))

    def finish(k):
        row = pl.ds(k, 1)
        skip = s_rows[row, :]
        x = x_ref[0, k]
        wide = x.astype(F32)
        state_low = srecv[k].astype(BF16)
        growth = g_cols[k]
        weights = w_cols[k]
        output = inner[k] + nn(c_ref[0], state_low) * growth
        error = output + skip * wide - t_ref[0, k].astype(F32)
        low = error.astype(BF16)
        gst[...] += nt(x, low) * decay[k]
        after = snext[k]
        adjoint = (urecv[k] + nn(wrecv[k], after, HIGHEST)).astype(BF16)
        grad = nn(mixed[k], low) + nn(b_ref[0], adjoint) * weights
        gx_ref[0, k] = (grad + skip * error).astype(BF16)
        gc_acc[...] += nt((error * growth).astype(BF16), state_low)
        gb_acc[...] += nt((wide * weights).astype(BF16), adjoint)
        pulled = wide * grad
        gl_rows[row, :] = row_sums(low.astype(F32) * output - pulled)
        cq_rows[row, :] = row_sums(pulled)
        gf_rows[row, :] = jnp.sum(adjoint.astype(F32) * after, axis=0, keepdims=True)
        sk_rows[row, :] = jnp.sum(error * wide, axis=0, keepdims=True)

    up, down = HOP
    s_at = (z * up) // down
    w_at = ((nz - 1 - z) * up) // down
    u_at = w_at + heads
    f_at = jnp.maximum(s_at, u_at)
    steps = ((nz - 1) * up) // down + 2 * heads

    def step(s, carry):
        def run(work, first):
            @pl.when(jnp.logical_and(s >= first, s < first + heads))
            def _():
                work(s - first)

        run(prepare, 0)
        run(pass_state, s_at)
        run(pass_gram, w_at)
        run(local, 0)
        run(pass_adjoint, u_at)
        run(finish, f_at)
        return carry

    lax.fori_loop(0, steps, step, 0)

    tokens = float(group * nz * ns)
    rising = nn(gl_rows[...], (iota((group, group), 0) >= iota((group, group), 1)).astype(F32), HIGHEST)
    rising = rising + jnp.sum(gf_rows[...], axis=1, keepdims=True)
    grad_raw = (cq_rows[...] / dt - rate * rising) * (1.0 / (1.0 + jnp.exp(-raw)))
    gdt_ref[0] = grad_raw
    totals = (
        jnp.sum(rising * dt, axis=1, keepdims=True) * (-rate / tokens),
        jnp.sum(sk_rows[...], axis=1, keepdims=True) / (tokens * width),
        jnp.sum(grad_raw, axis=1, keepdims=True) / tokens,
    )
    packed = jnp.zeros((heads, width), F32)
    for q, total in enumerate(totals):
        mine = iota((heads, width), 1) == iota((heads, width), 0) + q * heads
        packed = packed + jnp.where(mine, total, 0.0)
    pz_own[0] = jnp.sum(packed, axis=0, keepdims=True)

    def spread(name, at, count, source_of, target, sends, receives):
        copies = []
        for d in range(1, count):
            to = lax.rem(at + d, count)
            copies.append(
                pltpu.make_async_remote_copy(
                    src_ref=source_of(to),
                    dst_ref=target.at[d],
                    send_sem=sends.at[d],
                    recv_sem=receives.at[d],
                    device_id={name: to},
                    device_id_type=pl.DeviceIdType.MESH,
                )
            )
        for copy in copies:
            copy.start()
        return copies

    z_copies = spread("ctx", z, nz, lambda to: pz_own.at[0], pz, pz_ss, pz_rs)

    gs_low = gst[...].astype(BF16)
    grad_b = gb_acc[...] + nn(gs_low, c_ref[0])
    grad_c = gc_acc[...] + tn(gs_low, b_ref[0])
    rows = group // nh
    for r in range(nh):
        rs_send[r, 0:rows] = grad_b[r * rows : (r + 1) * rows]
        rs_send[r, rows : 2 * rows] = grad_c[r * rows : (r + 1) * rows]
    h_copies = spread("head", head_at, nh, lambda to: rs_send.at[to], rs_recv, rs_ss, rs_rs)

    total = pz_own[0]
    for d, copy in enumerate(z_copies, 1):
        copy.wait_recv()
        total = total + pz[d]
    px_own[0] = total
    x_copies = spread("seq", seq_at, ns, lambda to: px_own.at[0], px, px_ss, px_rs)

    whole = rs_send[head_at]
    for d, copy in enumerate(h_copies, 1):
        copy.wait_recv()
        whole = whole + rs_recv[d]
    gb_ref[0] = whole[0:rows]
    gc_ref[0] = whole[rows : 2 * rows]

    for d, copy in enumerate(x_copies, 1):
        copy.wait_recv()
        total = total + px[d]
    for q, out in enumerate((oalog_ref, oskip_ref, obias_ref)):
        turned = total if q == 0 else pltpu.roll(total, width - q * heads, 1)
        out[...] = turned[:, 0:heads]

    for copy in z_copies + h_copies + x_copies:
        copy.wait_send()

    def drain(k, carry):
        for part in range(PARTS):

            @pl.when(z < nz - 1)
            def _():
                s_copy(k, part).wait_send()

            @pl.when(z > 0)
            def _():
                w_copy(k, part).wait_send()
                u_copy(k, part).wait_send()

        return carry

    lax.fori_loop(0, heads, drain, 0)


def on_device(sizes, x, t, b, c, dt, a_log, skip, bias):
    nz, nh, ns = sizes
    _, heads, group, width = x.shape
    state = b.shape[2]
    rows = group // nh
    vmem = pl.BlockSpec(memory_space=pltpu.VMEM)
    whole = pltpu.VMEM((heads, state, width), F32)
    tall = pltpu.VMEM((heads, group, width), F32)
    line = pltpu.VMEM((heads, group), F32)
    short = pltpu.VMEM((heads, width), F32)
    flat = pltpu.VMEM((state, group), F32)
    square = pltpu.VMEM((group, group), F32)
    panel = pltpu.VMEM((group, width), F32)
    chain_sems = pltpu.SemaphoreType.DMA((heads * PARTS,))
    sems = [chain_sems] * 6
    for count in (nh, nz, ns):
        sems += [pltpu.SemaphoreType.DMA((count,))] * 2
    outs = pl.pallas_call(
        functools.partial(kernel, sizes),
        out_shape=(
            jax.ShapeDtypeStruct(x.shape, BF16),
            jax.ShapeDtypeStruct((1, rows, state), F32),
            jax.ShapeDtypeStruct((1, rows, state), F32),
            jax.ShapeDtypeStruct(dt.shape, F32),
        )
        + (jax.ShapeDtypeStruct((1, heads), F32),) * 3,
        in_specs=[vmem] * 8,
        out_specs=(vmem,) * 7,
        scratch_shapes=[line] * 4
        + [short] * 3
        + [line] * 2
        + [short] * 2
        + [
            flat,
            flat,
            square,
            pltpu.VMEM((state, group), BF16),
            pltpu.VMEM((heads, group, group), F32),
            pltpu.VMEM((heads, group, group), BF16),
            tall,
            tall,
            tall,
        ]
        + [whole] * 8
        + [
            square,
            panel,
            panel,
            pltpu.VMEM((nh, 2 * rows, width), F32),
            pltpu.VMEM((nh, 2 * rows, width), F32),
            pltpu.VMEM((nz, 1, width), F32),
            pltpu.VMEM((ns, 1, width), F32),
            pltpu.VMEM((1, 1, width), F32),
            pltpu.VMEM((1, 1, width), F32),
        ]
        + sems,
        compiler_params=pltpu.CompilerParams(collective_id=0, has_side_effects=True),
        name="mixer",
    )(x, t, b, c, dt, a_log.reshape(1, heads), skip.reshape(1, heads), bias.reshape(1, heads))
    return outs[:4] + tuple(o.reshape(heads) for o in outs[4:])


def solution(mesh):
    sizes = tuple(mesh.shape[name] for name in ("ctx", "head", "seq"))
    return jax.shard_map(
        functools.partial(on_device, sizes),
        mesh=mesh,
        in_specs=(
            P("seq", "head", "ctx", None),
            P("seq", "head", "ctx", None),
            P("seq", "ctx", None),
            P("seq", "ctx", None),
            P("seq", "head", "ctx"),
            P("head"),
            P("head"),
            P("head"),
        ),
        out_specs=(
            P("seq", "head", "ctx", None),
            P("seq", ("ctx", "head"), None),
            P("seq", ("ctx", "head"), None),
            P("seq", "head", "ctx"),
            P("head"),
            P("head"),
            P("head"),
        ),
        check_vma=False,
    )
```

```python
import functools
import math

import jax
import jax.numpy as jnp
from jax import lax
from jax.experimental import pallas as pl
from jax.experimental.pallas import tpu as pltpu
from jax.sharding import PartitionSpec as P

LOG2E = math.log2(math.e)
PARTS = 4
GRAM_PARTS = 2
HOP = (7, 4)
LATE = 5
F32 = jnp.float32
BF16 = jnp.bfloat16
HIGHEST = lax.Precision.HIGHEST


def nn(a, b, precision=None):
    return lax.dot_general(a, b, (((1,), (0,)), ((), ())), precision=precision, preferred_element_type=F32)


def nt(a, b):
    return lax.dot_general(a, b, (((1,), (1,)), ((), ())), preferred_element_type=F32)


def tn(a, b):
    return lax.dot_general(a, b, (((0,), (0,)), ((), ())), preferred_element_type=F32)


def iota(shape, dim):
    return lax.broadcasted_iota(jnp.int32, shape, dim)


def column(ref, heads):
    eye = iota((heads, heads), 0) == iota((heads, heads), 1)
    spread = jnp.broadcast_to(ref[...], (heads, heads))
    return jnp.sum(jnp.where(eye, spread, 0.0), axis=1, keepdims=True)


def row_sums(values):
    high = values.astype(BF16)
    low = (values - high.astype(F32)).astype(BF16)
    both = jnp.concatenate([high, low], axis=1)
    return nt(jnp.ones((8, both.shape[1]), BF16), both)[0:1]


def pack_gram(m):
    n = m.shape[0]
    q = n // 4
    lane = iota((q, n), 1)
    second = m[q : 2 * q]
    return (
        jnp.where(lane[: q // 2] < 2 * q, second[: q // 2], pltpu.roll(second[q // 2 :], 2 * q, 1)),
        jnp.where(lane < 3 * q, m[2 * q : 3 * q], pltpu.roll(m[:q], 3 * q, 1)),
        m[3 * q :],
    )


def unpack_gram(p):
    n = p.shape[1]
    q = n // 4
    half, third = p[: q // 2], p[q // 2 : q // 2 + q]
    lower = jnp.concatenate([pltpu.roll(third, q, 1), half, pltpu.roll(half, 2 * q, 1), third, p[q // 2 + q :]], axis=0)
    return jnp.where(iota((n, n), 0) // q >= iota((n, n), 1) // q, lower, lower.T)


def kernel(
    sizes, x_ref, t_ref, b_ref, c_ref, dt_ref, alog_ref, skip_ref, bias_ref,
    gx_ref, gb_ref, gc_ref, gdt_ref, sums_ref,
    l_rows, r_rows, w_rows, g_rows, d_rows, lt_rows, s_rows, gl_rows, cq_rows, gf_rows, sk_rows,
    bt, ct, scores, cgt, decay, mixed, inner, g_cols, w_cols, gx_part, gx_out,
    contrib, srecv, snext, gram, tbuf, vbuf, pbuf, urecv, mpack, wrecv,
    gst, gb_acc, gc_acc, rb_send, rb_recv, rc_send, rc_recv, pz, px, pz_own, px_own,
    s_send, s_recv, u_send, u_recv, w_send, w_recv,
    rb_ss, rb_rs, rc_ss, rc_rs, pz_ss, pz_rs, px_ss, px_rs, gx_sem,
):
    nz, nh, ns = sizes
    heads, group, width = x_ref.shape[1:]
    state = b_ref.shape[2]
    rows = group // nh
    z = lax.axis_index("ctx")
    head_at = lax.axis_index("head")
    seq_at = lax.axis_index("seq")

    barrier = pltpu.get_barrier_semaphore()

    def greet(name, to):
        pl.semaphore_signal(barrier, inc=1, device_id={name: to}, device_id_type=pl.DeviceIdType.MESH)

    @pl.when(z > 0)
    def _():
        greet("ctx", z - 1)

    @pl.when(z < nz - 1)
    def _():
        greet("ctx", z + 1)

    for name, at, count in (("head", head_at, nh), ("seq", seq_at, ns)):
        for d in range(1, count):
            greet(name, lax.rem(at + d, count))

    rate = jnp.exp(column(alog_ref, heads))
    bias = column(bias_ref, heads)
    raw = dt_ref[0] + bias
    dt = jnp.maximum(raw, 0.0) + jnp.log1p(jnp.exp(-jnp.abs(raw)))
    upper = (iota((group, group), 0) <= iota((group, group), 1)).astype(F32)
    logs = nn(dt * (rate * -LOG2E), upper, HIGHEST)
    last = logs[:, group - 1 : group]
    rel = jnp.log(dt) * LOG2E - logs
    l_rows[...] = logs
    r_rows[...] = rel
    w_rows[...] = jnp.exp2(last + rel)
    g_rows[...] = jnp.exp2(logs)
    d_rows[...] = jnp.broadcast_to(jnp.exp2(last), (heads, width))
    lt_rows[...] = jnp.broadcast_to(last, (heads, width))
    s_rows[...] = jnp.broadcast_to(column(skip_ref, heads), (heads, width))
    bt[...] = b_ref[0].astype(F32).T
    ct[...] = c_ref[0].astype(F32).T
    scores[...] = nt(b_ref[0], c_ref[0])
    gst[...] = jnp.zeros_like(gst)
    gb_acc[...] = jnp.zeros_like(gb_acc)
    gc_acc[...] = jnp.zeros_like(gc_acc)

    met = nh + ns - 2 + jnp.where(z > 0, 1, 0) + jnp.where(z < nz - 1, 1, 0)
    pl.semaphore_wait(barrier, met)

    def chain(source, target, sends, receives, k, part, parts, step):
        piece = source.shape[1] // parts
        at = pl.ds(part * piece, piece)
        return pltpu.make_async_remote_copy(
            src_ref=source.at[k, at],
            dst_ref=target.at[k, at],
            send_sem=sends.at[k * parts + part],
            recv_sem=receives.at[k * parts + part],
            device_id={"ctx": lax.rem(z + step, nz)},
            device_id_type=pl.DeviceIdType.MESH,
        )

    def s_copy(k, part):
        return chain(snext, srecv, s_send, s_recv, k, part, PARTS, 1)

    def w_copy(k, part):
        return chain(mpack, wrecv, w_send, w_recv, k, part, GRAM_PARTS, nz - 1)

    def u_copy(k, part):
        return chain(pbuf, urecv, u_send, u_recv, k, part, PARTS, nz - 1)

    def prepare(k):
        row = pl.ds(k, 1)
        contrib[k] = nn((bt[...] * w_rows[row, :]).astype(BF16), x_ref[0, k])
        scaled_c = (ct[...] * g_rows[row, :]).astype(BF16)
        cgt[k] = scaled_c
        at = 0
        for tile in pack_gram(nt(scaled_c, scaled_c)):
            mpack[k, at : at + tile.shape[0]] = tile
            at += tile.shape[0]

    def pass_state(k):
        d = d_rows[pl.ds(k, 1), :]
        for part in range(PARTS):
            at = pl.ds(part * (state // PARTS), state // PARTS)

            @pl.when(z > 0)
            def _():
                s_copy(k, part).wait_recv()
                snext[k, at] = d * srecv[k, at] + contrib[k, at]

            @pl.when(z == 0)
            def _():
                snext[k, at] = contrib[k, at]

            @pl.when(z < nz - 1)
            def _():
                s_copy(k, part).start()

        @pl.when(z == 0)
        def _():
            srecv[k] = jnp.zeros((state, width), F32)

    def pass_gram(k):
        d = d_rows[pl.ds(k, 1), :]
        piece = mpack.shape[1] // GRAM_PARTS
        for part in range(GRAM_PARTS):
            at = pl.ds(part * piece, piece)

            @pl.when(z < nz - 1)
            def _():
                w_copy(k, part).wait_recv()
                mpack[k, at] = (d * d) * wrecv[k, at] + mpack[k, at]

            @pl.when(z > 0)
            def _():
                w_copy(k, part).start()

        @pl.when(z < nz - 1)
        def _():
            full = unpack_gram(wrecv[k])
            gram[k] = full
            tbuf[k] = nn(full, contrib[k], HIGHEST)

        @pl.when(z == nz - 1)
        def _():
            gram[k] = jnp.zeros((state, state), F32)
            urecv[k] = jnp.zeros((state, width), F32)

    def pass_adjoint(k):
        d = d_rows[pl.ds(k, 1), :]
        for part in range(PARTS):
            at = pl.ds(part * (state // PARTS), state // PARTS)

            @pl.when(z < nz - 1)
            def _():
                u_copy(k, part).wait_recv()
                pbuf[k, at] = d * (urecv[k, at] + tbuf[k, at]) + pbuf[k, at]

            @pl.when(z > 0)
            def _():
                u_copy(k, part).start()

    def local(k):
        row = pl.ds(k, 1)
        logs_row = l_rows[row, :]
        rel_col = jnp.broadcast_to(r_rows[row, :], (width, group)).T
        logs_col = jnp.broadcast_to(logs_row, (width, group)).T
        g_cols[k] = jnp.exp2(logs_col)
        w_cols[k] = jnp.exp2(rel_col + lt_rows[row, :])
        gaps = jnp.concatenate([rel_col] * (group // width), axis=1) + logs_row
        causal = iota((group, group), 1) >= iota((group, group), 0)
        scaled_decay = jnp.exp2(jnp.where(causal, gaps, -1e30))
        decay[k] = scaled_decay
        mix = (scores[...] * scaled_decay).astype(BF16)
        mixed[k] = mix
        x = x_ref[0, k]
        within = tn(mix, x)
        inner[k] = within
        error = within + s_rows[row, :] * x.astype(F32) - t_ref[0, k].astype(F32)
        pbuf[k] = nn(cgt[k], error.astype(BF16))

    def cross(k):
        vbuf[k] = nn(gram[k], snext[k], HIGHEST)

    def forward(k):
        row = pl.ds(k, 1)
        skip = s_rows[row, :]
        x = x_ref[0, k]
        wide = x.astype(F32)
        state_low = srecv[k].astype(BF16)
        growth = g_cols[k]
        output = inner[k] + nn(c_ref[0], state_low) * growth
        error = output + skip * wide - t_ref[0, k].astype(F32)
        low = error.astype(BF16)
        gst[...] += nt(x, low) * decay[k]
        grad = nn(mixed[k], low)
        gx_part[k] = grad + skip * error
        gc_acc[...] += nt((error * growth).astype(BF16), state_low)
        pulled = wide * grad
        cq_rows[row, :] = row_sums(pulled)
        gl_rows[row, :] = row_sums(low.astype(F32) * output - pulled)
        sk_rows[row, :] = jnp.sum(error * wide, axis=0, keepdims=True)

    def backward(k):
        row = pl.ds(k, 1)
        wide = x_ref[0, k].astype(F32)
        weights = w_cols[k]
        adjoint = (urecv[k] + vbuf[k]).astype(BF16)
        grad = nn(b_ref[0], adjoint) * weights
        gx_out[k] = (gx_part[k] + grad).astype(BF16)
        gx_copy(k).start()
        gb_acc[...] += nt((wide * weights).astype(BF16), adjoint)
        sums = row_sums(wide * grad)
        gl_rows[row, :] = gl_rows[row, :] - sums
        cq_rows[row, :] = cq_rows[row, :] + sums
        gf_rows[row, :] = jnp.sum(adjoint.astype(F32) * snext[k], axis=0, keepdims=True)

    def gx_copy(k):
        return pltpu.make_async_copy(gx_out.at[k], gx_ref.at[0, k], gx_sem.at[k])

    def spread(name, at, count, source_of, target, sends, receives):
        copies = []
        for d in range(1, count):
            to = lax.rem(at + d, count)
            copies.append(
                pltpu.make_async_remote_copy(
                    src_ref=source_of(to),
                    dst_ref=target.at[d],
                    send_sem=sends.at[d],
                    recv_sem=receives.at[d],
                    device_id={name: to},
                    device_id_type=pl.DeviceIdType.MESH,
                )
            )
        return copies

    def c_spread():
        return spread("head", head_at, nh, lambda to: rc_send.at[to], rc_recv, rc_ss, rc_rs)

    def send_c(k):
        gs_low = gst[...].astype(BF16)
        gb_acc[...] += nn(gs_low, c_ref[0])
        grad_c = gc_acc[...] + tn(gs_low, b_ref[0])
        for r in range(nh):
            rc_send[r] = grad_c[r * rows : (r + 1) * rows]
        for copy in c_spread():
            copy.start()

    up, down = HOP
    back = nz - 1 - z
    s_at = (z * up) // down
    w_at = (back * up) // down + jnp.minimum(back, LATE)
    u_at = w_at + heads
    l_at = jnp.where(back < 3, heads, 0)
    steps = ((nz - 1) * up) // down + LATE + 2 * heads + 1

    def step(s, carry):
        def run(work, first, count=heads):
            @pl.when(jnp.logical_and(s >= first, s < first + count))
            def _():
                work(s - first)

        run(prepare, 0)
        run(pass_state, s_at)
        run(pass_gram, w_at)
        run(local, l_at)
        run(pass_adjoint, u_at)
        run(forward, jnp.maximum(s_at, l_at))
        run(cross, jnp.maximum(s_at, w_at))
        run(send_c, jnp.maximum(s_at, l_at) + heads, 1)
        run(backward, jnp.maximum(s_at, u_at))
        return carry

    lax.fori_loop(0, steps, step, 0)

    tokens = float(group * nz * ns)
    rising = nn(gl_rows[...], (iota((group, group), 0) >= iota((group, group), 1)).astype(F32), HIGHEST)
    rising = rising + jnp.sum(gf_rows[...], axis=1, keepdims=True)
    grad_raw = (cq_rows[...] / dt - rate * rising) * (1.0 / (1.0 + jnp.exp(-raw)))
    gdt_ref[0] = grad_raw
    totals = (
        jnp.sum(rising * dt, axis=1, keepdims=True) * (-rate / tokens),
        jnp.sum(sk_rows[...], axis=1, keepdims=True) / (tokens * width),
        jnp.sum(grad_raw, axis=1, keepdims=True) / tokens,
    )
    packed = jnp.zeros((heads, width), F32)
    for q, total in enumerate(totals):
        mine = iota((heads, width), 1) == iota((heads, width), 0) + q * heads
        packed = packed + jnp.where(mine, total, 0.0)
    pz_own[0] = jnp.sum(packed, axis=0, keepdims=True)
    z_copies = spread("ctx", z, nz, lambda to: pz_own.at[0], pz, pz_ss, pz_rs)
    for copy in z_copies:
        copy.start()

    for r in range(nh):
        rb_send[r] = gb_acc[r * rows : (r + 1) * rows]
    b_copies = spread("head", head_at, nh, lambda to: rb_send.at[to], rb_recv, rb_ss, rb_rs)
    for copy in b_copies:
        copy.start()

    def drain(k, carry):
        gx_copy(k).wait()
        for part in range(PARTS):

            @pl.when(z < nz - 1)
            def _():
                s_copy(k, part).wait_send()

            @pl.when(z > 0)
            def _():
                u_copy(k, part).wait_send()

        for part in range(GRAM_PARTS):

            @pl.when(z > 0)
            def _():
                w_copy(k, part).wait_send()

        return carry

    lax.fori_loop(0, heads, drain, 0)

    c_copies = c_spread()
    whole = rc_send[head_at]
    for d, copy in enumerate(c_copies, 1):
        copy.wait_recv()
        whole = whole + rc_recv[d]
    gc_ref[0] = whole

    total = pz_own[0]
    for d, copy in enumerate(z_copies, 1):
        copy.wait_recv()
        total = total + pz[d]
    px_own[0] = total
    x_copies = spread("seq", seq_at, ns, lambda to: px_own.at[0], px, px_ss, px_rs)
    for copy in x_copies:
        copy.start()

    whole = rb_send[head_at]
    for d, copy in enumerate(b_copies, 1):
        copy.wait_recv()
        whole = whole + rb_recv[d]
    gb_ref[0] = whole

    for d, copy in enumerate(x_copies, 1):
        copy.wait_recv()
        total = total + px[d]
    sums_ref[...] = total

    for copy in z_copies + b_copies + c_copies + x_copies:
        copy.wait_send()


def deliver(gx_in, gb_in, gc_in, gdt_in, sums_in, gx, gb, gc, gdt, alog, skip, bias, hold, into, out):
    heads = gx_in.shape[1]
    arrive = [pltpu.make_async_copy(gx_in.at[0, k], hold.at[k], into.at[k]) for k in range(heads)]
    leave = [pltpu.make_async_copy(hold.at[k], gx.at[0, k], out.at[k]) for k in range(heads)]
    for copy in arrive:
        copy.start()
    gb[...] = gb_in[...]
    gc[...] = gc_in[...]
    gdt[...] = gdt_in[...]
    sums = sums_in[...]
    for q, ref in enumerate((alog, skip, bias)):
        turned = sums if q == 0 else pltpu.roll(sums, sums.shape[1] - q * heads, 1)
        ref[...] = turned[:, 0:heads]
    for k in range(heads):
        arrive[k].wait()
        leave[k].start()
    for copy in leave:
        copy.wait()


def on_device(sizes, x, t, b, c, dt, a_log, skip, bias):
    nz, nh, ns = sizes
    _, heads, group, width = x.shape
    state = b.shape[2]
    rows = group // nh
    vmem = pl.BlockSpec(memory_space=pltpu.VMEM)
    anywhere = pl.BlockSpec(memory_space=pl.ANY)
    whole = pltpu.VMEM((heads, state, width), F32)
    tall = pltpu.VMEM((heads, group, width), F32)
    line = pltpu.VMEM((heads, group), F32)
    short = pltpu.VMEM((heads, width), F32)
    flat = pltpu.VMEM((state, group), F32)
    square = pltpu.VMEM((group, group), F32)
    panel = pltpu.VMEM((group, width), F32)
    packed = pltpu.VMEM((heads, state * 5 // 8, state), F32)
    slots = pltpu.VMEM((nh, rows, width), F32)
    sems = [pltpu.SemaphoreType.DMA((heads * PARTS,))] * 4 + [pltpu.SemaphoreType.DMA((heads * GRAM_PARTS,))] * 2
    for count in (nh, nh, nz, ns):
        sems += [pltpu.SemaphoreType.DMA((count,))] * 2
    sems += [pltpu.SemaphoreType.DMA((heads,))]
    gx_shape = jax.ShapeDtypeStruct(x.shape, BF16)
    part_shape = jax.ShapeDtypeStruct((1, rows, state), F32)
    dt_shape = jax.ShapeDtypeStruct(dt.shape, F32)
    head_shape = jax.ShapeDtypeStruct((1, heads), F32)
    parts = pl.pallas_call(
        functools.partial(kernel, sizes),
        out_shape=(gx_shape, part_shape, part_shape, dt_shape, jax.ShapeDtypeStruct((1, width), F32)),
        in_specs=[vmem] * 8,
        out_specs=(anywhere,) + (vmem,) * 4,
        scratch_shapes=[line] * 4
        + [short] * 3
        + [line] * 2
        + [short] * 2
        + [
            flat,
            flat,
            square,
            pltpu.VMEM((heads, state, group), BF16),
            pltpu.VMEM((heads, group, group), F32),
            pltpu.VMEM((heads, group, group), BF16),
            tall,
            tall,
            tall,
            tall,
            pltpu.VMEM((heads, group, width), BF16),
        ]
        + [whole] * 8
        + [packed] * 2
        + [square, panel, panel]
        + [slots] * 4
        + [
            pltpu.VMEM((nz, 1, width), F32),
            pltpu.VMEM((ns, 1, width), F32),
            pltpu.VMEM((1, 1, width), F32),
            pltpu.VMEM((1, 1, width), F32),
        ]
        + sems,
        compiler_params=pltpu.CompilerParams(collective_id=0, has_side_effects=True),
        name="mixer",
    )(x, t, b, c, dt, a_log.reshape(1, heads), skip.reshape(1, heads), bias.reshape(1, heads))
    outs = pl.pallas_call(
        deliver,
        out_shape=(gx_shape, part_shape, part_shape, dt_shape) + (head_shape,) * 3,
        in_specs=[anywhere] + [vmem] * 4,
        out_specs=(anywhere,) + (vmem,) * 6,
        scratch_shapes=[pltpu.VMEM((heads, group, width), BF16)] + [pltpu.SemaphoreType.DMA((heads,))] * 2,
        name="deliver",
    )(*parts)
    return outs[:4] + tuple(o.reshape(heads) for o in outs[4:])


def solution(mesh):
    sizes = tuple(mesh.shape[name] for name in ("ctx", "head", "seq"))
    return jax.shard_map(
        functools.partial(on_device, sizes),
        mesh=mesh,
        in_specs=(
            P("seq", "head", "ctx", None),
            P("seq", "head", "ctx", None),
            P("seq", "ctx", None),
            P("seq", "ctx", None),
            P("seq", "head", "ctx"),
            P("head"),
            P("head"),
            P("head"),
        ),
        out_specs=(
            P("seq", "head", "ctx", None),
            P("seq", ("ctx", "head"), None),
            P("seq", ("ctx", "head"), None),
            P("seq", "head", "ctx"),
            P("head"),
            P("head"),
            P("head"),
        ),
        check_vma=False,
    )
```

```python
import functools
import math

import jax
import jax.numpy as jnp
from jax import lax
from jax.experimental import pallas as pl
from jax.experimental.pallas import tpu as pltpu
from jax.sharding import PartitionSpec as P

LOG2E = math.log2(math.e)
PARTS = 4
GRAM_PARTS = 2
HOP = 8
LATE = 10
SOON, NEAR, FAR = 3, 7, 12
F32 = jnp.float32
BF16 = jnp.bfloat16
HIGHEST = lax.Precision.HIGHEST


def nn(a, b, precision=None):
    return lax.dot_general(a, b, (((1,), (0,)), ((), ())), precision=precision, preferred_element_type=F32)


def nt(a, b):
    return lax.dot_general(a, b, (((1,), (1,)), ((), ())), preferred_element_type=F32)


def tn(a, b):
    return lax.dot_general(a, b, (((0,), (0,)), ((), ())), preferred_element_type=F32)


def iota(shape, dim):
    return lax.broadcasted_iota(jnp.int32, shape, dim)


def column(ref, heads):
    eye = iota((heads, heads), 0) == iota((heads, heads), 1)
    spread = jnp.broadcast_to(ref[...], (heads, heads))
    return jnp.sum(jnp.where(eye, spread, 0.0), axis=1, keepdims=True)


def row_sums(values):
    high = values.astype(BF16)
    low = (values - high.astype(F32)).astype(BF16)
    both = jnp.concatenate([high, low], axis=1)
    return nt(jnp.ones((8, both.shape[1]), BF16), both)[0:1]


def pack_gram(m):
    n = m.shape[0]
    q = n // 4
    lane = iota((q, n), 1)
    second = m[q : 2 * q]
    return (
        jnp.where(lane[: q // 2] < 2 * q, second[: q // 2], pltpu.roll(second[q // 2 :], 2 * q, 1)),
        jnp.where(lane < 3 * q, m[2 * q : 3 * q], pltpu.roll(m[:q], 3 * q, 1)),
        m[3 * q :],
    )


def unpack_gram(p):
    n = p.shape[1]
    q = n // 4
    half, third = p[: q // 2], p[q // 2 : q // 2 + q]
    lower = jnp.concatenate([pltpu.roll(third, q, 1), half, pltpu.roll(half, 2 * q, 1), third, p[q // 2 + q :]], axis=0)
    return jnp.where(iota((n, n), 0) // q >= iota((n, n), 1) // q, lower, lower.T)


def plan(z, nz, heads, where, most):
    back = nz - 1 - z
    span = heads * PARTS
    grams = heads * GRAM_PARTS
    soon, near, far = z < nz * SOON // 16, z < nz * NEAR // 16, z >= nz * FAR // 16
    s_at = z * HOP
    w_at = back * HOP + where(back > 0, LATE, 0)
    u_at = w_at + grams + grams // 4
    both = most(s_at, u_at)
    l_at = where(soon, s_at + span, where(far, u_at - PARTS, 2 * heads))
    l_by = where(far, PARTS, 2)
    f_at = most(where(soon, l_at, where(near, s_at, both) + PARTS - 1), l_at)
    f_by = where(soon, 2, PARTS)
    inside = most(w_at + GRAM_PARTS - 1, s_at + span // 2 + 1)
    c_at = where(near, inside, where(far, both + PARTS - 1, both + span))
    c_by = where(near, GRAM_PARTS, where(far, PARTS, 2))
    b_at = most(where(near, both + PARTS - 1, where(far, both + PARTS - 1, both + span)), most(c_at, f_at))
    b_by = where(near, PARTS, where(far, PARTS, 2))
    return s_at, w_at, u_at, l_at, l_by, f_at, f_by, c_at, c_by, b_at, b_by, b_at + heads * PARTS + 2


def kernel(
    sizes, x_in, t_in, b_in, c_in, dt_in, alog_in, skip_in, bias_in,
    gx_ref, gb_out, gc_out, gdt_out, sums_out,
    x_ref, t_ref, b_ref, c_ref, dt_ref, alog_ref, skip_ref, bias_ref, gb_ref, gc_ref, gdt_ref, sums_ref,
    l_rows, r_rows, w_rows, g_rows, d_rows, lt_rows, s_rows, gl_rows, cq_rows, gf_rows, sk_rows,
    bt, ct, scores, cgt, decay, mixed, inner, g_cols, w_cols, gx_part, gx_out,
    contrib, srecv, snext, gram, tbuf, vbuf, pbuf, urecv, mpack, wrecv,
    gst, gb_acc, gc_acc, rb_send, rb_recv, rc_send, rc_recv, pz, px, pz_own, px_own,
    s_send, s_recv, u_send, u_recv, w_send, w_recv,
    rb_ss, rb_rs, rc_ss, rc_rs, pz_ss, pz_rs, px_ss, px_rs, gx_sem, in_sem, out_sem,
):
    nz, nh, ns = sizes
    heads, group, width = x_ref.shape[1:]
    state = b_ref.shape[2]
    rows = group // nh
    z = lax.axis_index("ctx")
    head_at = lax.axis_index("head")
    seq_at = lax.axis_index("seq")

    barrier = pltpu.get_barrier_semaphore()

    def greet(name, to):
        pl.semaphore_signal(barrier, inc=1, device_id={name: to}, device_id_type=pl.DeviceIdType.MESH)

    @pl.when(z > 0)
    def _():
        greet("ctx", z - 1)

    @pl.when(z < nz - 1)
    def _():
        greet("ctx", z + 1)

    for name, at, count in (("head", head_at, nh), ("seq", seq_at, ns)):
        for d in range(1, count):
            greet(name, lax.rem(at + d, count))

    pairs = (
        (dt_in, dt_ref), (alog_in, alog_ref), (bias_in, bias_ref), (skip_in, skip_ref),
        (b_in, b_ref), (c_in, c_ref), (x_in, x_ref), (t_in, t_ref),
    )
    arriving = [pltpu.make_async_copy(source, target, in_sem.at[i]) for i, (source, target) in enumerate(pairs)]
    for copy in arriving:
        copy.start()
    for copy in arriving[:6]:
        copy.wait()

    rate = jnp.exp(column(alog_ref, heads))
    bias = column(bias_ref, heads)
    raw = dt_ref[0] + bias
    dt = jnp.maximum(raw, 0.0) + jnp.log1p(jnp.exp(-jnp.abs(raw)))
    upper = (iota((group, group), 0) <= iota((group, group), 1)).astype(F32)
    logs = nn(dt * (rate * -LOG2E), upper, HIGHEST)
    last = logs[:, group - 1 : group]
    rel = jnp.log(dt) * LOG2E - logs
    l_rows[...] = logs
    r_rows[...] = rel
    w_rows[...] = jnp.exp2(last + rel)
    g_rows[...] = jnp.exp2(logs)
    d_rows[...] = jnp.broadcast_to(jnp.exp2(last), (heads, width))
    lt_rows[...] = jnp.broadcast_to(last, (heads, width))
    s_rows[...] = jnp.broadcast_to(column(skip_ref, heads), (heads, width))
    bt[...] = b_ref[0].astype(F32).T
    ct[...] = c_ref[0].astype(F32).T
    scores[...] = nt(b_ref[0], c_ref[0])
    gst[...] = jnp.zeros_like(gst)
    gb_acc[...] = jnp.zeros_like(gb_acc)
    gc_acc[...] = jnp.zeros_like(gc_acc)

    for copy in arriving[6:]:
        copy.wait()
    met = nh + ns - 2 + jnp.where(z > 0, 1, 0) + jnp.where(z < nz - 1, 1, 0)
    pl.semaphore_wait(barrier, met)

    def chain(source, target, sends, receives, k, part, parts, step):
        piece = source.shape[1] // parts
        at = pl.ds(pl.multiple_of(part * piece, piece), piece)
        return pltpu.make_async_remote_copy(
            src_ref=source.at[k, at],
            dst_ref=target.at[k, at],
            send_sem=sends.at[k * parts + part],
            recv_sem=receives.at[k * parts + part],
            device_id={"ctx": lax.rem(z + step, nz)},
            device_id_type=pl.DeviceIdType.MESH,
        )

    def s_copy(k, part):
        return chain(snext, srecv, s_send, s_recv, k, part, PARTS, 1)

    def w_copy(k, part):
        return chain(mpack, wrecv, w_send, w_recv, k, part, GRAM_PARTS, nz - 1)

    def u_copy(k, part):
        return chain(pbuf, urecv, u_send, u_recv, k, part, PARTS, nz - 1)

    def prepare(k):
        row = pl.ds(k, 1)
        contrib[k] = nn((bt[...] * w_rows[row, :]).astype(BF16), x_ref[0, k])
        scaled_c = (ct[...] * g_rows[row, :]).astype(BF16)
        cgt[k] = scaled_c
        at = 0
        for tile in pack_gram(nt(scaled_c, scaled_c)):
            mpack[k, at : at + tile.shape[0]] = tile
            at += tile.shape[0]

    def pass_state(p):
        k = p // PARTS
        part = lax.rem(p, PARTS)
        d = d_rows[pl.ds(k, 1), :]
        at = pl.ds(pl.multiple_of(part * (state // PARTS), state // PARTS), state // PARTS)

        @pl.when(z > 0)
        def _():
            s_copy(k, part).wait_recv()
            snext[k, at] = d * srecv[k, at] + contrib[k, at]

        @pl.when(z == 0)
        def _():
            snext[k, at] = contrib[k, at]
            srecv[k, at] = jnp.zeros((state // PARTS, width), F32)

        @pl.when(z < nz - 1)
        def _():
            s_copy(k, part).start()

    def pass_gram(q):
        k = q // GRAM_PARTS
        part = lax.rem(q, GRAM_PARTS)
        d = d_rows[pl.ds(k, 1), :]
        piece = mpack.shape[1] // GRAM_PARTS
        at = pl.ds(pl.multiple_of(part * piece, piece), piece)

        @pl.when(z < nz - 1)
        def _():
            w_copy(k, part).wait_recv()
            mpack[k, at] = (d * d) * wrecv[k, at] + mpack[k, at]

        @pl.when(z > 0)
        def _():
            w_copy(k, part).start()

    def widen(k):
        @pl.when(z < nz - 1)
        def _():
            full = unpack_gram(wrecv[k])
            gram[k] = full
            tbuf[k] = nn(full, contrib[k], HIGHEST)

        @pl.when(z == nz - 1)
        def _():
            gram[k] = jnp.zeros((state, state), F32)
            urecv[k] = jnp.zeros((state, width), F32)

    def pass_adjoint(p):
        k = p // PARTS
        part = lax.rem(p, PARTS)
        d = d_rows[pl.ds(k, 1), :]
        at = pl.ds(pl.multiple_of(part * (state // PARTS), state // PARTS), state // PARTS)

        @pl.when(z < nz - 1)
        def _():
            u_copy(k, part).wait_recv()
            pbuf[k, at] = d * (urecv[k, at] + tbuf[k, at]) + pbuf[k, at]

        @pl.when(z > 0)
        def _():
            u_copy(k, part).start()

    def local(k):
        row = pl.ds(k, 1)
        logs_row = l_rows[row, :]
        rel_col = jnp.broadcast_to(r_rows[row, :], (width, group)).T
        logs_col = jnp.broadcast_to(logs_row, (width, group)).T
        g_cols[k] = jnp.exp2(logs_col)
        w_cols[k] = jnp.exp2(rel_col + lt_rows[row, :])
        gaps = jnp.concatenate([rel_col] * (group // width), axis=1) + logs_row
        causal = iota((group, group), 1) >= iota((group, group), 0)
        scaled_decay = jnp.exp2(jnp.where(causal, gaps, -1e30))
        decay[k] = scaled_decay
        mix = (scores[...] * scaled_decay).astype(BF16)
        mixed[k] = mix
        x = x_ref[0, k]
        within = tn(mix, x)
        inner[k] = within
        error = within + s_rows[row, :] * x.astype(F32) - t_ref[0, k].astype(F32)
        pbuf[k] = nn(cgt[k], error.astype(BF16))

    def cross(k):
        vbuf[k] = nn(gram[k], snext[k], HIGHEST)

    def forward(k):
        row = pl.ds(k, 1)
        skip = s_rows[row, :]
        x = x_ref[0, k]
        wide = x.astype(F32)
        state_low = srecv[k].astype(BF16)
        growth = g_cols[k]
        output = inner[k] + nn(c_ref[0], state_low) * growth
        error = output + skip * wide - t_ref[0, k].astype(F32)
        low = error.astype(BF16)
        gst[...] += nt(x, low) * decay[k]
        grad = nn(mixed[k], low)
        gx_part[k] = grad + skip * error
        gc_acc[...] += nt((error * growth).astype(BF16), state_low)
        pulled = wide * grad
        cq_rows[row, :] = row_sums(pulled)
        gl_rows[row, :] = row_sums(low.astype(F32) * output - pulled)
        sk_rows[row, :] = jnp.sum(error * wide, axis=0, keepdims=True)

    def backward(k):
        row = pl.ds(k, 1)
        wide = x_ref[0, k].astype(F32)
        weights = w_cols[k]
        adjoint = (urecv[k] + vbuf[k]).astype(BF16)
        grad = nn(b_ref[0], adjoint) * weights
        gx_out[k] = (gx_part[k] + grad).astype(BF16)
        gx_copy(k).start()
        gb_acc[...] += nt((wide * weights).astype(BF16), adjoint)
        sums = row_sums(wide * grad)
        gl_rows[row, :] = gl_rows[row, :] - sums
        cq_rows[row, :] = cq_rows[row, :] + sums
        gf_rows[row, :] = jnp.sum(adjoint.astype(F32) * snext[k], axis=0, keepdims=True)

    def gx_copy(k):
        return pltpu.make_async_copy(gx_out.at[k], gx_ref.at[0, k], gx_sem.at[k])

    def spread(name, at, count, source_of, target, sends, receives):
        copies = []
        for d in range(1, count):
            to = lax.rem(at + d, count)
            copies.append(
                pltpu.make_async_remote_copy(
                    src_ref=source_of(to),
                    dst_ref=target.at[d],
                    send_sem=sends.at[d],
                    recv_sem=receives.at[d],
                    device_id={name: to},
                    device_id_type=pl.DeviceIdType.MESH,
                )
            )
        return copies

    def c_spread():
        return spread("head", head_at, nh, lambda to: rc_send.at[to], rc_recv, rc_ss, rc_rs)

    def send_c(k):
        gs_low = gst[...].astype(BF16)
        gb_acc[...] += nn(gs_low, c_ref[0])
        grad_c = gc_acc[...] + tn(gs_low, b_ref[0])
        for r in range(nh):
            rc_send[r] = grad_c[r * rows : (r + 1) * rows]
        for copy in c_spread():
            copy.start()

    s_at, w_at, u_at, l_at, l_by, f_at, f_by, c_at, c_by, b_at, b_by, _ = plan(z, nz, heads, jnp.where, jnp.maximum)
    span = heads * PARTS
    grams = heads * GRAM_PARTS
    steps = max(plan(at, nz, heads, lambda c, x, y: x if c else y, max)[-1] for at in range(nz))

    def step(s, carry):
        def relay(work, first, count):
            @pl.when(jnp.logical_and(s >= first, s < first + count))
            def _():
                work(s - first)

        def run(work, first, by, count=heads):
            past = s - first

            @pl.when(jnp.logical_and(past >= 0, jnp.logical_and(past < by * count, lax.rem(past, by) == 0)))
            def _():
                work(past // by)

        run(prepare, 0, 2)
        relay(pass_gram, w_at, grams)
        run(widen, w_at + GRAM_PARTS - 1, GRAM_PARTS)
        run(local, l_at, l_by)
        relay(pass_adjoint, u_at, span)
        relay(pass_state, s_at, span)
        run(forward, f_at, f_by)
        run(cross, c_at, c_by)
        run(backward, b_at, b_by)
        run(send_c, f_at + f_by * heads, 1, 1)
        return carry

    lax.fori_loop(0, steps, step, 0)

    tokens = float(group * nz * ns)
    rising = nn(gl_rows[...], (iota((group, group), 0) >= iota((group, group), 1)).astype(F32), HIGHEST)
    rising = rising + jnp.sum(gf_rows[...], axis=1, keepdims=True)
    grad_raw = (cq_rows[...] / dt - rate * rising) * (1.0 / (1.0 + jnp.exp(-raw)))
    gdt_ref[0] = grad_raw
    gdt_copy = pltpu.make_async_copy(gdt_ref, gdt_out, out_sem.at[0])
    gdt_copy.start()
    totals = (
        jnp.sum(rising * dt, axis=1, keepdims=True) * (-rate / tokens),
        jnp.sum(sk_rows[...], axis=1, keepdims=True) / (tokens * width),
        jnp.sum(grad_raw, axis=1, keepdims=True) / tokens,
    )
    packed = jnp.zeros((heads, width), F32)
    for q, total in enumerate(totals):
        mine = iota((heads, width), 1) == iota((heads, width), 0) + q * heads
        packed = packed + jnp.where(mine, total, 0.0)
    pz_own[0] = jnp.sum(packed, axis=0, keepdims=True)
    z_copies = spread("ctx", z, nz, lambda to: pz_own.at[0], pz, pz_ss, pz_rs)
    for copy in z_copies:
        copy.start()

    for r in range(nh):
        rb_send[r] = gb_acc[r * rows : (r + 1) * rows]
    b_copies = spread("head", head_at, nh, lambda to: rb_send.at[to], rb_recv, rb_ss, rb_rs)
    for copy in b_copies:
        copy.start()

    def drain(k, carry):
        gx_copy(k).wait()
        for part in range(PARTS):

            @pl.when(z < nz - 1)
            def _():
                s_copy(k, part).wait_send()

            @pl.when(z > 0)
            def _():
                u_copy(k, part).wait_send()

        for part in range(GRAM_PARTS):

            @pl.when(z > 0)
            def _():
                w_copy(k, part).wait_send()

        return carry

    lax.fori_loop(0, heads, drain, 0)

    c_copies = c_spread()
    whole = rc_send[head_at]
    for d, copy in enumerate(c_copies, 1):
        copy.wait_recv()
        whole = whole + rc_recv[d]
    gc_ref[0] = whole
    gc_copy = pltpu.make_async_copy(gc_ref, gc_out, out_sem.at[1])
    gc_copy.start()

    total = pz_own[0]
    for d, copy in enumerate(z_copies, 1):
        copy.wait_recv()
        total = total + pz[d]
    px_own[0] = total
    x_copies = spread("seq", seq_at, ns, lambda to: px_own.at[0], px, px_ss, px_rs)
    for copy in x_copies:
        copy.start()

    whole = rb_send[head_at]
    for d, copy in enumerate(b_copies, 1):
        copy.wait_recv()
        whole = whole + rb_recv[d]
    gb_ref[0] = whole
    gb_copy = pltpu.make_async_copy(gb_ref, gb_out, out_sem.at[2])
    gb_copy.start()

    for d, copy in enumerate(x_copies, 1):
        copy.wait_recv()
        total = total + px[d]
    sums_ref[...] = total
    sums_copy = pltpu.make_async_copy(sums_ref, sums_out, out_sem.at[3])
    sums_copy.start()

    for copy in z_copies + b_copies + c_copies + x_copies:
        copy.wait_send()
    for copy in (gdt_copy, gc_copy, gb_copy, sums_copy):
        copy.wait()


def deliver(*refs):
    ins, outs, (gx, gb, gc, gdt, sums_ref, *heads_refs), (into, out) = refs[:5], refs[5:12], refs[12:20], refs[20:]
    heads = gx.shape[1]
    held = (gx, gb, gc, gdt)
    arrive = [pltpu.make_async_copy(ins[4], sums_ref, into.at[4])]
    arrive += [pltpu.make_async_copy(a, b, into.at[i]) for i, (a, b) in enumerate(zip(ins[:4], held))]
    for copy in arrive:
        copy.start()
    arrive[0].wait()
    sums = sums_ref[...]
    for q, ref in enumerate(heads_refs):
        turned = sums if q == 0 else pltpu.roll(sums, sums.shape[1] - q * heads, 1)
        ref[...] = turned[:, 0:heads]
    leave = [pltpu.make_async_copy(a, b, out.at[i]) for i, (a, b) in enumerate(zip(held + tuple(heads_refs), outs))]
    for copy in leave[4:]:
        copy.start()
    for i in range(4):
        arrive[i + 1].wait()
        leave[i].start()
    for copy in leave:
        copy.wait()


def on_device(sizes, x, t, b, c, dt, a_log, skip, bias):
    nz, nh, ns = sizes
    _, heads, group, width = x.shape
    state = b.shape[2]
    rows = group // nh
    anywhere = pl.BlockSpec(memory_space=pl.ANY)
    whole = pltpu.VMEM((heads, state, width), F32)
    tall = pltpu.VMEM((heads, group, width), F32)
    line = pltpu.VMEM((heads, group), F32)
    short = pltpu.VMEM((heads, width), F32)
    flat = pltpu.VMEM((state, group), F32)
    square = pltpu.VMEM((group, group), F32)
    panel = pltpu.VMEM((group, width), F32)
    packed = pltpu.VMEM((heads, state * 5 // 8, state), F32)
    slots = pltpu.VMEM((nh, rows, width), F32)
    sems = [pltpu.SemaphoreType.DMA((heads * PARTS,))] * 4 + [pltpu.SemaphoreType.DMA((heads * GRAM_PARTS,))] * 2
    for count in (nh, nh, nz, ns):
        sems += [pltpu.SemaphoreType.DMA((count,))] * 2
    sems += [pltpu.SemaphoreType.DMA((count,)) for count in (heads, 8, 4)]
    gx_shape = jax.ShapeDtypeStruct(x.shape, BF16)
    part_shape = jax.ShapeDtypeStruct((1, rows, state), F32)
    dt_shape = jax.ShapeDtypeStruct(dt.shape, F32)
    head_shape = jax.ShapeDtypeStruct((1, heads), F32)
    parts = pl.pallas_call(
        functools.partial(kernel, sizes),
        out_shape=(gx_shape, part_shape, part_shape, dt_shape, jax.ShapeDtypeStruct((1, width), F32)),
        in_specs=[anywhere] * 8,
        out_specs=(anywhere,) * 5,
        scratch_shapes=[pltpu.VMEM(a.shape, a.dtype) for a in (x, t, b, c, dt)]
        + [pltpu.VMEM((1, heads), F32)] * 3
        + [pltpu.VMEM((1, rows, state), F32)] * 2
        + [pltpu.VMEM(dt.shape, F32), pltpu.VMEM((1, width), F32)]
        + [line] * 4
        + [short] * 3
        + [line] * 2
        + [short] * 2
        + [
            flat,
            flat,
            square,
            pltpu.VMEM((heads, state, group), BF16),
            pltpu.VMEM((heads, group, group), F32),
            pltpu.VMEM((heads, group, group), BF16),
            tall,
            tall,
            tall,
            tall,
            pltpu.VMEM((heads, group, width), BF16),
        ]
        + [whole] * 8
        + [packed] * 2
        + [square, panel, panel]
        + [slots] * 4
        + [
            pltpu.VMEM((nz, 1, width), F32),
            pltpu.VMEM((ns, 1, width), F32),
            pltpu.VMEM((1, 1, width), F32),
            pltpu.VMEM((1, 1, width), F32),
        ]
        + sems,
        compiler_params=pltpu.CompilerParams(collective_id=0, has_side_effects=True),
        name="mixer",
    )(x, t, b, c, dt, a_log.reshape(1, heads), skip.reshape(1, heads), bias.reshape(1, heads))
    outs = pl.pallas_call(
        deliver,
        out_shape=(gx_shape, part_shape, part_shape, dt_shape) + (head_shape,) * 3,
        in_specs=[anywhere] * 5,
        out_specs=(anywhere,) * 7,
        scratch_shapes=[pltpu.VMEM(a.shape, a.dtype) for a in parts]
        + [pltpu.VMEM((1, heads), F32)] * 3
        + [pltpu.SemaphoreType.DMA((5,)), pltpu.SemaphoreType.DMA((7,))],
        name="deliver",
    )(*parts)
    return outs[:4] + tuple(o.reshape(heads) for o in outs[4:])


def solution(mesh):
    sizes = tuple(mesh.shape[name] for name in ("ctx", "head", "seq"))
    return jax.shard_map(
        functools.partial(on_device, sizes),
        mesh=mesh,
        in_specs=(
            P("seq", "head", "ctx", None),
            P("seq", "head", "ctx", None),
            P("seq", "ctx", None),
            P("seq", "ctx", None),
            P("seq", "head", "ctx"),
            P("head"),
            P("head"),
            P("head"),
        ),
        out_specs=(
            P("seq", "head", "ctx", None),
            P("seq", ("ctx", "head"), None),
            P("seq", ("ctx", "head"), None),
            P("seq", "head", "ctx"),
            P("head"),
            P("head"),
            P("head"),
        ),
        check_vma=False,
    )
```

```python
import functools
import math

import jax
import jax.numpy as jnp
from jax import lax
from jax.experimental import pallas as pl
from jax.experimental.pallas import tpu as pltpu
from jax.sharding import PartitionSpec as P

LOG2E = math.log2(math.e)
PARTS = 4
GRAM_PARTS = 2
SLOTS = 2
HOP = 9
LATE = 5
SOON, NEAR, FAR = 3, 7, 12
F32 = jnp.float32
BF16 = jnp.bfloat16
HIGHEST = lax.Precision.HIGHEST


def nn(a, b, precision=None):
    return lax.dot_general(a, b, (((1,), (0,)), ((), ())), precision=precision, preferred_element_type=F32)


def nt(a, b):
    return lax.dot_general(a, b, (((1,), (1,)), ((), ())), preferred_element_type=F32)


def tn(a, b):
    return lax.dot_general(a, b, (((0,), (0,)), ((), ())), preferred_element_type=F32)


def iota(shape, dim):
    return lax.broadcasted_iota(jnp.int32, shape, dim)


def column(ref, heads):
    eye = iota((heads, heads), 0) == iota((heads, heads), 1)
    spread = jnp.broadcast_to(ref[...], (heads, heads))
    return jnp.sum(jnp.where(eye, spread, 0.0), axis=1, keepdims=True)


def row_sums(values):
    high = values.astype(BF16)
    low = (values - high.astype(F32)).astype(BF16)
    both = jnp.concatenate([high, low], axis=1)
    return nt(jnp.ones((8, both.shape[1]), BF16), both)[0:1]


def pack_gram(m):
    n = m.shape[0]
    q = n // 4
    lane = iota((q, n), 1)
    second = m[q : 2 * q]
    return (
        jnp.where(lane[: q // 2] < 2 * q, second[: q // 2], pltpu.roll(second[q // 2 :], 2 * q, 1)),
        jnp.where(lane < 3 * q, m[2 * q : 3 * q], pltpu.roll(m[:q], 3 * q, 1)),
        m[3 * q :],
    )


def unpack_gram(p):
    n = p.shape[1]
    q = n // 4
    half, third = p[: q // 2], p[q // 2 : q // 2 + q]
    lower = jnp.concatenate([pltpu.roll(third, q, 1), half, pltpu.roll(half, 2 * q, 1), third, p[q // 2 + q :]], axis=0)
    return jnp.where(iota((n, n), 0) // q >= iota((n, n), 1) // q, lower, lower.T)


def plan(z, nz, heads, where, most):
    back = nz - 1 - z
    span = heads * SLOTS
    soon, near, far = z < nz * SOON // 16, z < nz * NEAR // 16, z >= nz * FAR // 16
    s_at = z * HOP // 2
    w_at = back * HOP // 2 + where(back > 0, LATE, 0)
    u_at = w_at + heads + heads // 4
    both = most(s_at, u_at)
    l_at = where(soon, s_at + span, where(far, u_at - SLOTS, heads))
    l_by = where(far, SLOTS, 1)
    f_at = most(where(soon, l_at, where(near, s_at, both) + SLOTS - 1), l_at)
    f_by = where(soon, 1, SLOTS)
    inside = most(w_at, s_at + span)
    c_at = where(near, inside, where(far, both + SLOTS - 1, both + span))
    c_by = where(far, SLOTS, 1)
    b_at = most(where(near, both + SLOTS - 1, where(far, both + SLOTS - 1, both + span)), most(c_at, f_at))
    b_by = where(near, SLOTS, where(far, SLOTS, 1))
    return s_at, w_at, u_at, l_at, l_by, f_at, f_by, c_at, c_by, b_at, b_by, b_at + b_by * (heads - 1) + 1, f_at + f_by * heads + 1


def kernel(
    sizes, x_in, t_in, b_in, c_in, dt_in, alog_in, skip_in, bias_in,
    gx_ref, gb_out, gc_out, gdt_out, sums_out,
    x_ref, t_ref, b_ref, c_ref, dt_ref, alog_ref, skip_ref, bias_ref, gb_ref, gc_ref, gdt_ref, sums_ref,
    l_rows, r_rows, w_rows, g_rows, d_rows, lt_rows, s_rows, gl_rows, cq_rows, gf_rows, sk_rows,
    bt, ct, scores, cgt, decay, mixed, inner, g_cols, w_cols, gx_part, gx_out,
    contrib, srecv, snext, gram, tbuf, vbuf, pbuf, urecv, mpack, wrecv,
    gst, gb_acc, gc_acc, rb_send, rb_recv, rc_send, rc_recv, pz, px, pz_own, px_own,
    s_send, s_recv, u_send, u_recv, w_send, w_recv,
    rb_ss, rb_rs, rc_ss, rc_rs, pz_ss, pz_rs, px_ss, px_rs, gx_sem, in_sem, out_sem,
):
    nz, nh, ns = sizes
    heads, group, width = x_ref.shape[1:]
    state = b_ref.shape[2]
    rows = group // nh
    z = lax.axis_index("ctx")
    head_at = lax.axis_index("head")
    seq_at = lax.axis_index("seq")

    barrier = pltpu.get_barrier_semaphore()

    def greet(name, to):
        pl.semaphore_signal(barrier, inc=1, device_id={name: to}, device_id_type=pl.DeviceIdType.MESH)

    @pl.when(z > 0)
    def _():
        greet("ctx", z - 1)

    @pl.when(z < nz - 1)
    def _():
        greet("ctx", z + 1)

    for name, at, count in (("head", head_at, nh), ("seq", seq_at, ns)):
        for d in range(1, count):
            greet(name, lax.rem(at + d, count))

    pairs = (
        (dt_in, dt_ref), (alog_in, alog_ref), (bias_in, bias_ref), (skip_in, skip_ref),
        (b_in, b_ref), (c_in, c_ref), (x_in, x_ref), (t_in, t_ref),
    )
    arriving = [pltpu.make_async_copy(source, target, in_sem.at[i]) for i, (source, target) in enumerate(pairs)]
    for copy in arriving:
        copy.start()
    for copy in arriving[:6]:
        copy.wait()

    rate = jnp.exp(column(alog_ref, heads))
    bias = column(bias_ref, heads)
    raw = dt_ref[0] + bias
    dt = jnp.maximum(raw, 0.0) + jnp.log1p(jnp.exp(-jnp.abs(raw)))
    upper = (iota((group, group), 0) <= iota((group, group), 1)).astype(F32)
    logs = nn(dt * (rate * -LOG2E), upper, HIGHEST)
    last = logs[:, group - 1 : group]
    rel = jnp.log(dt) * LOG2E - logs
    l_rows[...] = logs
    r_rows[...] = rel
    w_rows[...] = jnp.exp2(last + rel)
    g_rows[...] = jnp.exp2(logs)
    d_rows[...] = jnp.broadcast_to(jnp.exp2(last), (heads, width))
    lt_rows[...] = jnp.broadcast_to(last, (heads, width))
    s_rows[...] = jnp.broadcast_to(column(skip_ref, heads), (heads, width))
    bt[...] = b_ref[0].astype(F32).T
    ct[...] = c_ref[0].astype(F32).T
    scores[...] = nt(b_ref[0], c_ref[0])
    gst[...] = jnp.zeros_like(gst)
    gb_acc[...] = jnp.zeros_like(gb_acc)
    gc_acc[...] = jnp.zeros_like(gc_acc)

    for copy in arriving[6:]:
        copy.wait()
    def prepare(k):
        row = pl.ds(k, 1)
        scaled_c = (ct[...] * g_rows[row, :]).astype(BF16)
        cgt[k] = scaled_c
        at = 0
        for tile in pack_gram(nt(scaled_c, scaled_c)):
            mpack[k, at : at + tile.shape[0]] = tile
            at += tile.shape[0]
        contrib[k] = nn((bt[...] * w_rows[row, :]).astype(BF16), x_ref[0, k])

    prepare(0)

    met = nh + ns - 2 + jnp.where(z > 0, 1, 0) + jnp.where(z < nz - 1, 1, 0)
    pl.semaphore_wait(barrier, met)

    def chain(source, target, sends, receives, k, part, parts, step):
        piece = source.shape[1] // parts
        at = pl.ds(pl.multiple_of(part * piece, piece), piece)
        return pltpu.make_async_remote_copy(
            src_ref=source.at[k, at],
            dst_ref=target.at[k, at],
            send_sem=sends.at[k * parts + part],
            recv_sem=receives.at[k * parts + part],
            device_id={"ctx": lax.rem(z + step, nz)},
            device_id_type=pl.DeviceIdType.MESH,
        )

    def s_copy(k, part):
        return chain(snext, srecv, s_send, s_recv, k, part, PARTS, 1)

    def w_copy(k, part):
        return chain(mpack, wrecv, w_send, w_recv, k, part, GRAM_PARTS, nz - 1)

    def u_copy(k, part):
        return chain(pbuf, urecv, u_send, u_recv, k, part, PARTS, nz - 1)

    def pass_state(p):
        k = p // SLOTS
        d = d_rows[pl.ds(k, 1), :]
        for sub in range(PARTS // SLOTS):
            part = lax.rem(p, SLOTS) * (PARTS // SLOTS) + sub
            at = pl.ds(pl.multiple_of(part * (state // PARTS), state // PARTS), state // PARTS)

            @pl.when(z > 0)
            def _():
                s_copy(k, part).wait_recv()
                snext[k, at] = d * srecv[k, at] + contrib[k, at]

            @pl.when(z == 0)
            def _():
                snext[k, at] = contrib[k, at]
                srecv[k, at] = jnp.zeros((state // PARTS, width), F32)

            @pl.when(z < nz - 1)
            def _():
                s_copy(k, part).start()

    def pass_gram(k):
        d = d_rows[pl.ds(k, 1), :]
        piece = mpack.shape[1] // GRAM_PARTS
        for part in range(GRAM_PARTS):
            at = pl.ds(part * piece, piece)

            @pl.when(z < nz - 1)
            def _():
                w_copy(k, part).wait_recv()
                mpack[k, at] = (d * d) * wrecv[k, at] + mpack[k, at]

            @pl.when(z > 0)
            def _():
                w_copy(k, part).start()

    def widen(k):
        @pl.when(z < nz - 1)
        def _():
            full = unpack_gram(wrecv[k])
            gram[k] = full
            tbuf[k] = nn(full, contrib[k], HIGHEST)

        @pl.when(z == nz - 1)
        def _():
            gram[k] = jnp.zeros((state, state), F32)
            urecv[k] = jnp.zeros((state, width), F32)

    def pass_adjoint(p):
        k = p // SLOTS
        d = d_rows[pl.ds(k, 1), :]
        for sub in range(PARTS // SLOTS):
            part = lax.rem(p, SLOTS) * (PARTS // SLOTS) + sub
            at = pl.ds(pl.multiple_of(part * (state // PARTS), state // PARTS), state // PARTS)

            @pl.when(z == 0)
            def _():
                u_copy(k, part).wait_recv()

            @pl.when(jnp.logical_and(z > 0, z < nz - 1))
            def _():
                u_copy(k, part).wait_recv()
                pbuf[k, at] = d * (urecv[k, at] + tbuf[k, at]) + pbuf[k, at]

            @pl.when(z > 0)
            def _():
                u_copy(k, part).start()

    def local(k):
        row = pl.ds(k, 1)
        logs_row = l_rows[row, :]
        rel_col = jnp.broadcast_to(r_rows[row, :], (width, group)).T
        logs_col = jnp.broadcast_to(logs_row, (width, group)).T
        g_cols[k] = jnp.exp2(logs_col)
        w_cols[k] = jnp.exp2(rel_col + lt_rows[row, :])
        gaps = jnp.concatenate([rel_col] * (group // width), axis=1) + logs_row
        causal = iota((group, group), 1) >= iota((group, group), 0)
        scaled_decay = jnp.exp2(jnp.where(causal, gaps, -1e30))
        decay[k] = scaled_decay
        mix = (scores[...] * scaled_decay).astype(BF16)
        mixed[k] = mix
        x = x_ref[0, k]
        within = tn(mix, x)
        inner[k] = within
        error = within + s_rows[row, :] * x.astype(F32) - t_ref[0, k].astype(F32)
        pbuf[k] = nn(cgt[k], error.astype(BF16))

    def cross(k):
        vbuf[k] = nn(gram[k], snext[k], HIGHEST)

    def forward(k):
        row = pl.ds(k, 1)
        skip = s_rows[row, :]
        x = x_ref[0, k]
        wide = x.astype(F32)
        state_low = srecv[k].astype(BF16)
        growth = g_cols[k]
        output = inner[k] + nn(c_ref[0], state_low) * growth
        error = output + skip * wide - t_ref[0, k].astype(F32)
        low = error.astype(BF16)
        gst[...] += nt(x, low) * decay[k]
        grad = nn(mixed[k], low)
        gx_part[k] = grad + skip * error
        gc_acc[...] += nt((error * growth).astype(BF16), state_low)
        pulled = wide * grad
        cq_rows[row, :] = row_sums(pulled)
        gl_rows[row, :] = row_sums(low.astype(F32) * output - pulled)
        sk_rows[row, :] = jnp.sum(error * wide, axis=0, keepdims=True)

    def backward(k):
        row = pl.ds(k, 1)
        wide = x_ref[0, k].astype(F32)
        weights = w_cols[k]
        adjoint = (urecv[k] + vbuf[k]).astype(BF16)
        grad = nn(b_ref[0], adjoint) * weights
        gx_out[k] = (gx_part[k] + grad).astype(BF16)
        gx_copy(k).start()
        gb_acc[...] += nt((wide * weights).astype(BF16), adjoint)
        sums = row_sums(wide * grad)
        gl_rows[row, :] = gl_rows[row, :] - sums
        cq_rows[row, :] = cq_rows[row, :] + sums
        gf_rows[row, :] = jnp.sum(adjoint.astype(F32) * snext[k], axis=0, keepdims=True)

    def gx_copy(k):
        return pltpu.make_async_copy(gx_out.at[k], gx_ref.at[0, k], gx_sem.at[k])

    def spread(name, at, count, source_of, target, sends, receives):
        copies = []
        for d in sorted(range(1, count), key=lambda d: abs(2 * d - count)):
            to = lax.rem(at + d, count)
            copies.append(
                pltpu.make_async_remote_copy(
                    src_ref=source_of(to),
                    dst_ref=target.at[d],
                    send_sem=sends.at[d],
                    recv_sem=receives.at[d],
                    device_id={name: to},
                    device_id_type=pl.DeviceIdType.MESH,
                )
            )
        return copies

    def c_spread():
        return spread("head", head_at, nh, lambda to: rc_send.at[to], rc_recv, rc_ss, rc_rs)

    def send_c(k):
        gs_low = gst[...].astype(BF16)
        gb_acc[...] += nn(gs_low, c_ref[0])
        grad_c = gc_acc[...] + tn(gs_low, b_ref[0])
        for r in range(nh):
            rc_send[r] = grad_c[r * rows : (r + 1) * rows]
        for copy in c_spread():
            copy.start()

    s_at, w_at, u_at, l_at, l_by, f_at, f_by, c_at, c_by, b_at, b_by, *_ = plan(z, nz, heads, jnp.where, jnp.maximum)
    span = heads * SLOTS
    steps = max(max(plan(at, nz, heads, lambda c, x, y: x if c else y, max)[-2:]) for at in range(nz))

    def step(s, carry):
        def relay(work, first, count):
            @pl.when(jnp.logical_and(s >= first, s < first + count))
            def _():
                work(s - first)

        def times(by):
            return SLOTS // by if isinstance(by, int) else jnp.where(by == SLOTS, 1, SLOTS)

        def run(work, first, by, count=heads):
            past = (s - first) * times(by)

            @pl.when(jnp.logical_and(past >= 0, jnp.logical_and(past < SLOTS * count, lax.rem(past, SLOTS) == 0)))
            def _():
                work(past // SLOTS)

        relay(lambda k: prepare(k + 1), 0, heads - 1)
        relay(pass_gram, w_at, heads)
        relay(widen, w_at, heads)
        run(local, l_at, l_by)
        relay(pass_adjoint, u_at, span)
        relay(pass_state, s_at, span)
        run(forward, f_at, f_by)
        run(cross, c_at, c_by)
        run(backward, b_at, b_by)
        run(send_c, f_at + f_by * heads, 1, 1)
        return carry

    lax.fori_loop(0, steps, step, 0)

    for r in range(nh):
        rb_send[r] = gb_acc[r * rows : (r + 1) * rows]
    b_copies = spread("head", head_at, nh, lambda to: rb_send.at[to], rb_recv, rb_ss, rb_rs)
    for copy in b_copies:
        copy.start()

    tokens = float(group * nz * ns)
    rising = nn(gl_rows[...], (iota((group, group), 0) >= iota((group, group), 1)).astype(F32), HIGHEST)
    rising = rising + jnp.sum(gf_rows[...], axis=1, keepdims=True)
    grad_raw = (cq_rows[...] / dt - rate * rising) * (1.0 / (1.0 + jnp.exp(-raw)))
    gdt_ref[0] = grad_raw
    gdt_copy = pltpu.make_async_copy(gdt_ref, gdt_out, out_sem.at[0])
    gdt_copy.start()
    totals = (
        jnp.sum(rising * dt, axis=1, keepdims=True) * (-rate / tokens),
        jnp.sum(sk_rows[...], axis=1, keepdims=True) / (tokens * width),
        jnp.sum(grad_raw, axis=1, keepdims=True) / tokens,
    )
    packed = jnp.zeros((heads, width), F32)
    for q, total in enumerate(totals):
        mine = iota((heads, width), 1) == iota((heads, width), 0) + q * heads
        packed = packed + jnp.where(mine, total, 0.0)
    pz_own[0] = jnp.sum(packed, axis=0, keepdims=True)
    z_copies = spread("ctx", z, nz, lambda to: pz_own.at[0], pz, pz_ss, pz_rs)
    for copy in z_copies:
        copy.start()

    def drain(k, carry):
        gx_copy(k).wait()
        for part in range(PARTS):

            @pl.when(z < nz - 1)
            def _():
                s_copy(k, part).wait_send()

            @pl.when(z > 0)
            def _():
                u_copy(k, part).wait_send()

        for part in range(GRAM_PARTS):

            @pl.when(z > 0)
            def _():
                w_copy(k, part).wait_send()

        return carry

    lax.fori_loop(0, heads, drain, 0)

    c_copies = c_spread()
    whole = rc_send[head_at]
    for copy in c_copies:
        copy.wait_recv()
    for d in range(1, nh):
        whole = whole + rc_recv[d]
    gc_ref[0] = whole
    gc_copy = pltpu.make_async_copy(gc_ref, gc_out, out_sem.at[1])
    gc_copy.start()

    total = pz_own[0]
    for copy in z_copies:
        copy.wait_recv()
    for d in range(1, nz):
        total = total + pz[d]
    px_own[0] = total
    x_copies = spread("seq", seq_at, ns, lambda to: px_own.at[0], px, px_ss, px_rs)
    for copy in x_copies:
        copy.start()

    whole = rb_send[head_at]
    for copy in b_copies:
        copy.wait_recv()
    for d in range(1, nh):
        whole = whole + rb_recv[d]
    gb_ref[0] = whole
    gb_copy = pltpu.make_async_copy(gb_ref, gb_out, out_sem.at[2])
    gb_copy.start()

    for copy in x_copies:
        copy.wait_recv()
    for d in range(1, ns):
        total = total + px[d]
    sums_ref[...] = total
    sums_copy = pltpu.make_async_copy(sums_ref, sums_out, out_sem.at[3])
    sums_copy.start()

    for copy in z_copies + b_copies + c_copies + x_copies:
        copy.wait_send()
    for copy in (gdt_copy, gc_copy, gb_copy, sums_copy):
        copy.wait()


def deliver(*refs):
    ins, outs, (gx, gb, gc, gdt, sums_ref, *heads_refs), (into, out) = refs[:5], refs[5:12], refs[12:20], refs[20:]
    heads = gx.shape[1]
    held = (gx, gb, gc, gdt)
    arrive = [pltpu.make_async_copy(ins[4], sums_ref, into.at[4])]
    arrive += [pltpu.make_async_copy(a, b, into.at[i]) for i, (a, b) in enumerate(zip(ins[:4], held))]
    for copy in arrive:
        copy.start()
    arrive[0].wait()
    sums = sums_ref[...]
    for q, ref in enumerate(heads_refs):
        turned = sums if q == 0 else pltpu.roll(sums, sums.shape[1] - q * heads, 1)
        ref[...] = turned[:, 0:heads]
    leave = [pltpu.make_async_copy(a, b, out.at[i]) for i, (a, b) in enumerate(zip(held + tuple(heads_refs), outs))]
    for copy in leave[4:]:
        copy.start()
    for i in range(4):
        arrive[i + 1].wait()
        leave[i].start()
    for copy in leave:
        copy.wait()


def on_device(sizes, x, t, b, c, dt, a_log, skip, bias):
    nz, nh, ns = sizes
    _, heads, group, width = x.shape
    state = b.shape[2]
    rows = group // nh
    anywhere = pl.BlockSpec(memory_space=pl.ANY)
    whole = pltpu.VMEM((heads, state, width), F32)
    tall = pltpu.VMEM((heads, group, width), F32)
    line = pltpu.VMEM((heads, group), F32)
    short = pltpu.VMEM((heads, width), F32)
    flat = pltpu.VMEM((state, group), F32)
    square = pltpu.VMEM((group, group), F32)
    panel = pltpu.VMEM((group, width), F32)
    packed = pltpu.VMEM((heads, state * 5 // 8, state), F32)
    slots = pltpu.VMEM((nh, rows, width), F32)
    sems = [pltpu.SemaphoreType.DMA((heads * PARTS,))] * 4 + [pltpu.SemaphoreType.DMA((heads * GRAM_PARTS,))] * 2
    for count in (nh, nh, nz, ns):
        sems += [pltpu.SemaphoreType.DMA((count,))] * 2
    sems += [pltpu.SemaphoreType.DMA((count,)) for count in (heads, 8, 4)]
    gx_shape = jax.ShapeDtypeStruct(x.shape, BF16)
    part_shape = jax.ShapeDtypeStruct((1, rows, state), F32)
    dt_shape = jax.ShapeDtypeStruct(dt.shape, F32)
    head_shape = jax.ShapeDtypeStruct((1, heads), F32)
    parts = pl.pallas_call(
        functools.partial(kernel, sizes),
        out_shape=(gx_shape, part_shape, part_shape, dt_shape, jax.ShapeDtypeStruct((1, width), F32)),
        in_specs=[anywhere] * 8,
        out_specs=(anywhere,) * 5,
        scratch_shapes=[pltpu.VMEM(a.shape, a.dtype) for a in (x, t, b, c, dt)]
        + [pltpu.VMEM((1, heads), F32)] * 3
        + [pltpu.VMEM((1, rows, state), F32)] * 2
        + [pltpu.VMEM(dt.shape, F32), pltpu.VMEM((1, width), F32)]
        + [line] * 4
        + [short] * 3
        + [line] * 2
        + [short] * 2
        + [
            flat,
            flat,
            square,
            pltpu.VMEM((heads, state, group), BF16),
            pltpu.VMEM((heads, group, group), F32),
            pltpu.VMEM((heads, group, group), BF16),
            tall,
            tall,
            tall,
            tall,
            pltpu.VMEM((heads, group, width), BF16),
        ]
        + [whole] * 8
        + [packed] * 2
        + [square, panel, panel]
        + [slots] * 4
        + [
            pltpu.VMEM((nz, 1, width), F32),
            pltpu.VMEM((ns, 1, width), F32),
            pltpu.VMEM((1, 1, width), F32),
            pltpu.VMEM((1, 1, width), F32),
        ]
        + sems,
        compiler_params=pltpu.CompilerParams(collective_id=0, has_side_effects=True),
        name="mixer",
    )(x, t, b, c, dt, a_log.reshape(1, heads), skip.reshape(1, heads), bias.reshape(1, heads))
    outs = pl.pallas_call(
        deliver,
        out_shape=(gx_shape, part_shape, part_shape, dt_shape) + (head_shape,) * 3,
        in_specs=[anywhere] * 5,
        out_specs=(anywhere,) * 7,
        scratch_shapes=[pltpu.VMEM(a.shape, a.dtype) for a in parts]
        + [pltpu.VMEM((1, heads), F32)] * 3
        + [pltpu.SemaphoreType.DMA((5,)), pltpu.SemaphoreType.DMA((7,))],
        name="deliver",
    )(*parts)
    return outs[:4] + tuple(o.reshape(heads) for o in outs[4:])


def solution(mesh):
    sizes = tuple(mesh.shape[name] for name in ("ctx", "head", "seq"))
    return jax.shard_map(
        functools.partial(on_device, sizes),
        mesh=mesh,
        in_specs=(
            P("seq", "head", "ctx", None),
            P("seq", "head", "ctx", None),
            P("seq", "ctx", None),
            P("seq", "ctx", None),
            P("seq", "head", "ctx"),
            P("head"),
            P("head"),
            P("head"),
        ),
        out_specs=(
            P("seq", "head", "ctx", None),
            P("seq", ("ctx", "head"), None),
            P("seq", ("ctx", "head"), None),
            P("seq", "head", "ctx"),
            P("head"),
            P("head"),
            P("head"),
        ),
        check_vma=False,
    )
```
